256 devices in a mesh: face: 8 (over y, x_lo), tile: 32 (over x_hi, z, core).
Axes of the slice: x: 4 (x_hi: 2, x_lo: 2; x = x_hi * 2 + x_lo), y: 4, z: 8, core: 2. Of those that a mesh axis runs over, the one named last changes fastest.
Arguments:
- fields: bfloat16 [8, 256, 128, 256], P('face', 'tile'), may hold values from -6 to 6
- cotangent: bfloat16 [8, 256, 128, 256], P('face', 'tile'), may hold values from -6 to 6
- edge_match: int32 [8, 2, 3], replicated, may hold values from 0 to 7, as said below
- depth_kernel: bfloat16 [7, 7, 256], replicated, may hold values from -0.875 to 0.875
- depth_bias: float32 [256], replicated, may hold values from -3 to 3
- norm_gain: float32 [256], replicated, may hold values from 0.5 to 1.5
- norm_bias: float32 [256], replicated, may hold values from -3 to 3
- expand_weight: bfloat16 [256, 1024], replicated, may hold values from -0.375 to 0.375
- expand_bias: float32 [1024], replicated, may hold values from -3 to 3
- reduce_weight: bfloat16 [1024, 256], replicated, may hold values from -0.1875 to 0.1875
- reduce_bias: float32 [256], replicated, may hold values from -3 to 3
- layer_scale: float32 [256], replicated, may hold values from 0.5 to 1.5
Outputs:
- result: bfloat16 [8, 256, 128, 256], P('face', 'tile')
- grad_fields: bfloat16 [8, 256, 128, 256], P('face', 'tile')
- grad_kernel: float32 [7, 7, 256], replicated
- grad_expand: float32 [256, 1024], replicated
- grad_reduce: float32 [1024, 256], replicated
- grad_expand_bias: float32 [1024], replicated
- grad_vectors: float32 [5, 256], replicated
The draws below stay inside these ranges and needn't reach their ends.
Inputs may be any that keep to these rules, and one draw needn't show every extreme that they name: edge_match[f, s] = (g, s2, r): side s of strip f is glued to side s2 of strip g, rows reversed where r is 1; the gluing is symmetric; one side of strip f is glued to strip f XOR 1, the other to strip (f + 4) mod 8; at least one glued pair has reversed rows and at least one has not.
All inputs are finite; a program needn't handle non-finite values.
Results may differ from the reference program's by a relative error of at most 0.0067.
Values may be sent and summed in bfloat16 or wider, within the bound.
A program may use at most 64 MiB of HBM per device.

```python
import math
import jax
import jax.numpy as jnp
from jax import lax

C = 256
HID = 1024
K = 7
FW = 128
FACES = 8
ROWS = 256
CELLS = 262144


def draw_edge_match(key, part):
    faces = jnp.arange(FACES, dtype=jnp.int32)
    first_side = jax.random.randint(jax.random.fold_in(key, 3), (FACES,), 0, 2).astype(jnp.int32)
    pair_flags = jax.random.randint(jax.random.fold_in(key, 5), (FACES,), 0, 2).astype(jnp.int32)
    forced_on = jax.random.randint(jax.random.fold_in(key, 7), (), 0, FACES).astype(jnp.int32)
    forced_off = (forced_on + 1 + jax.random.randint(jax.random.fold_in(key, 9), (), 0, FACES - 1).astype(jnp.int32)) % FACES
    pair_flags = jnp.where(faces == forced_on, 1, jnp.where(faces == forced_off, 0, pair_flags)).astype(jnp.int32)
    half_count = FACES // 2
    across = (faces + half_count) % FACES
    beside = jnp.bitwise_xor(faces, 1)
    across_row = jnp.stack([across, first_side[across], pair_flags[jnp.minimum(faces, across)]], axis=1)
    beside_row = jnp.stack([beside, 1 - first_side[beside], pair_flags[half_count + jnp.minimum(faces, beside) // 2]], axis=1)
    side_zero = jnp.where((first_side == 0)[:, None], across_row, beside_row)
    side_one = jnp.where((first_side == 1)[:, None], across_row, beside_row)
    return jnp.stack([side_zero, side_one], axis=1).astype(jnp.int32)


def block_scale(stream_key, shape, pieces, smallest, high):
    def one(dim, blocks):
        steps = jax.random.uniform(jax.random.fold_in(jax.random.fold_in(stream_key, 6), dim), (blocks,), jnp.float32, smallest / len(pieces), high / len(pieces))
        return jnp.repeat(jnp.exp(steps), shape[dim] // blocks).reshape((-1,) + (1,) * (len(shape) - dim - 1))

    gain = one(*pieces[0])
    for cut in pieces[1:]:
        gain = gain * one(*cut)
    return gain


def noise(key, dims, scale, bound, pieces=(), kind=jnp.bfloat16):
    level = block_scale(key, dims, pieces, -0.22, 0.18) if pieces else 1.0
    values = jax.random.normal(key, dims, jnp.float32) * scale * level
    return jnp.minimum(jnp.maximum(values, -bound), bound).astype(kind)


def setup_inputs(seed: int = 0) -> dict:
    key_of = jax.random.split(jax.random.key(seed), 13)
    return {
        "fields": noise(key_of[0], (FACES, ROWS, FW, C), 1.0, 6.0, ((0, 8), (1, 32))),
        "cotangent": noise(key_of[1], (FACES, ROWS, FW, C), 1.0, 6.0, ((0, 8), (1, 32))),
        "edge_match": draw_edge_match(jax.random.fold_in(key_of[12], 71), 0),
        "depth_kernel": noise(key_of[3], (K, K, C), (K * K) ** -0.5, 0.875),
        "depth_bias": noise(key_of[4], (C,), 0.5, 3.0, (), jnp.float32),
        "norm_gain": jnp.clip(jax.random.uniform(key_of[5], (C,), jnp.float32, 0.5, 1.5), 0.5, 1.5),
        "norm_bias": noise(key_of[6], (C,), 0.5, 3.0, (), jnp.float32),
        "expand_weight": noise(key_of[7], (C, HID), C ** -0.5, 0.375),
        "expand_bias": noise(key_of[8], (HID,), 0.5, 3.0, (), jnp.float32),
        "reduce_weight": noise(key_of[9], (HID, C), HID ** -0.5, 0.1875),
        "reduce_bias": noise(key_of[10], (C,), 0.5, 3.0, (), jnp.float32),
        "layer_scale": jnp.clip(jax.random.uniform(key_of[11], (C,), jnp.float32, 0.5, 1.5), 0.5, 1.5),
    }


EPSILON = 1e-06
ROOT_COEF = 0.7978845608028654
CUBIC_COEF = 0.044715

def gelu_pair(preact):
    argument = ROOT_COEF * (preact + CUBIC_COEF * preact * preact * preact)
    tanhed = jnp.tanh(argument)
    gelu_value = 0.5 * preact * (1.0 + tanhed)
    gelu_slope = 0.5 * (1.0 + tanhed) + 0.5 * preact * (1.0 - tanhed * tanhed) * ROOT_COEF * (1.0 + 3.0 * CUBIC_COEF * preact * preact)
    return (gelu_value, gelu_slope)

def contract_rows(left_side, right_side):
    return lax.dot_general(left_side, right_side, (((0,), (0,)), ((), ())), preferred_element_type=jnp.float32)

def contract_cols(left_side, right_side):
    return lax.dot_general(left_side, right_side, (((1,), (1,)), ((), ())), preferred_element_type=jnp.float32)

def block_pass(padded, face_grid, face_cot, kernel, depth_bias, norm_gain, norm_bias, expand_weight, expand_bias, reduce_weight, reduce_bias, layer_scale):
    row_count, col_count, channels = face_grid.shape
    kernel_size = kernel.shape[0]
    convolved = jnp.zeros((row_count, col_count, channels), jnp.float32) + depth_bias
    for row_off in range(kernel_size):
        for col_off in range(kernel_size):
            convolved = convolved + kernel[row_off, col_off] * padded[row_off:row_off + row_count, col_off:col_off + col_count]
    average = lax.optimization_barrier(jnp.mean(convolved, axis=-1, keepdims=True))
    centred = convolved - average
    inverse = lax.rsqrt(lax.optimization_barrier(jnp.mean(centred * centred, axis=-1, keepdims=True)) + EPSILON)
    standard = centred * inverse
    normed = (standard * norm_gain + norm_bias).astype(jnp.bfloat16).reshape(row_count * col_count, channels)
    preact = jnp.dot(normed, expand_weight, preferred_element_type=jnp.float32) + expand_bias
    gelu_value, gelu_slope = gelu_pair(preact)
    activated = gelu_value.astype(jnp.bfloat16)
    branch = jnp.dot(activated, reduce_weight, preferred_element_type=jnp.float32) + reduce_bias
    residual = face_grid.reshape(row_count * col_count, channels).astype(jnp.float32)
    result = (residual + layer_scale * branch).astype(jnp.bfloat16).reshape(row_count, col_count, channels)
    upstream = face_cot.reshape(row_count * col_count, channels).astype(jnp.float32)
    grad_branch = (upstream * layer_scale).astype(jnp.bfloat16)
    grad_pre = (contract_cols(grad_branch, reduce_weight) * gelu_slope).astype(jnp.bfloat16)
    grad_normed = contract_cols(grad_pre, expand_weight).reshape(row_count, col_count, channels)
    scaled = grad_normed * norm_gain
    grad_conv = (scaled - lax.optimization_barrier(jnp.mean(scaled, axis=-1, keepdims=True)) - standard * lax.optimization_barrier(jnp.mean(scaled * standard, axis=-1, keepdims=True))) * inverse
    dz_padded = jnp.pad(grad_conv, ((6, 6), (6, 6), (0, 0)))
    grad_padded = jnp.zeros((row_count + 6, col_count + 6, channels), jnp.float32)
    kernel_terms = []
    for row_off in range(kernel_size):
        for col_off in range(kernel_size):
            grad_padded = grad_padded + kernel[row_off, col_off] * dz_padded[6 - row_off:12 - row_off + row_count, 6 - col_off:12 - col_off + col_count]
            kernel_terms.append(lax.optimization_barrier(jnp.sum(grad_conv * padded[row_off:row_off + row_count, col_off:col_off + col_count], axis=(0, 1))))
    grad_kernel = jnp.stack(kernel_terms).reshape(kernel_size, kernel_size, channels)
    grad_expand = contract_rows(normed, grad_pre)
    grad_reduce = contract_rows(activated, grad_branch)
    grad_expand_bias = lax.optimization_barrier(jnp.sum(grad_pre.astype(jnp.float32), axis=0))
    vectors = jnp.stack([lax.optimization_barrier(jnp.sum(grad_conv, axis=(0, 1))), lax.optimization_barrier(jnp.sum(grad_normed * standard, axis=(0, 1))), lax.optimization_barrier(jnp.sum(grad_normed, axis=(0, 1))), lax.optimization_barrier(jnp.sum(upstream, axis=0)) * layer_scale, lax.optimization_barrier(jnp.sum(upstream * branch, axis=0))])
    return (result, grad_padded, (grad_kernel, grad_expand, grad_reduce, grad_expand_bias, vectors))

def edge_depths(grids):
    west_side = grids[:, :, 0:3]
    east_side = jnp.flip(grids[:, :, FW - 3:], 2)
    return jnp.stack([west_side, east_side], axis=1)

def glue(depths, edge_match):
    chosen = depths[edge_match[:, :, 0], edge_match[:, :, 1]]
    reverse_flag = edge_match[:, :, 2][:, :, None, None, None]
    return jnp.where(reverse_flag == 1, jnp.flip(chosen, 2), chosen)

def reference(fields, cotangent, edge_match, depth_kernel, depth_bias, norm_gain, norm_bias, expand_weight, expand_bias, reduce_weight, reduce_bias, layer_scale):
    ghost_all = glue(edge_depths(fields), edge_match)
    kernel = depth_kernel.astype(jnp.float32)

    def face_step(totals, face_item):
        face_grid, face_cot, ghosts = face_item
        widened = jnp.concatenate([jnp.flip(ghosts[0], 1), face_grid, ghosts[1]], axis=1)
        padded = jnp.pad(widened, ((3, 3), (0, 0), (0, 0))).astype(jnp.float32)
        result, grad_padded, terms = block_pass(padded, face_grid, face_cot, kernel, depth_bias, norm_gain, norm_bias, expand_weight, expand_bias, reduce_weight, reduce_bias, layer_scale)
        interior = face_cot.astype(jnp.float32) + grad_padded[3:ROWS + 3, 3:FW + 3]
        ghost_grads = jnp.stack([jnp.flip(grad_padded[3:ROWS + 3, 0:3], 1), grad_padded[3:ROWS + 3, FW + 3:FW + 6]])
        totals = tuple((total + term for total, term in zip(totals, terms)))
        return (totals, (result, interior, ghost_grads))
    zero_totals = (jnp.zeros((K, K, C), jnp.float32), jnp.zeros((C, HID), jnp.float32), jnp.zeros((HID, C), jnp.float32), jnp.zeros((HID,), jnp.float32), jnp.zeros((5, C), jnp.float32))
    totals, (results, interior, ghost_grads) = lax.scan(face_step, zero_totals, (fields, cotangent, ghost_all))
    returned = glue(ghost_grads, edge_match)
    interior = interior.at[:, :, 0:3].add(returned[:, 0])
    interior = interior.at[:, :, FW - 3:].add(jnp.flip(returned[:, 1], 2))
    factor = 1.0 / math.sqrt(CELLS)
    return (results, interior.astype(jnp.bfloat16), totals[0] * factor, totals[1] * factor, totals[2] * factor, totals[3] * factor, totals[4] * factor)
```

```python
import functools
import math

import jax
import jax.numpy as jnp
from jax import lax
from jax.experimental import pallas as pl
from jax.experimental.pallas import tpu as pltpu
from jax.sharding import PartitionSpec as P

EPSILON = 1e-06
ROOT_COEF = 0.7978845608028654
CUBIC_COEF = 0.044715
MESH = pl.DeviceIdType.MESH
FACES = 8
TILES = 32
F32 = jnp.float32
BF16 = jnp.bfloat16


def halo_plan(face, tile):
    beside = face + 1 - 2 * lax.rem(face, 2)
    across = lax.rem(face + 4, FACES)
    plan = [
        ("up", (face, lax.rem(tile + TILES - 1, TILES))),
        ("down", (face, lax.rem(tile + 1, TILES))),
    ]
    for link, partner in enumerate((beside, across)):
        for flip in range(2):
            for place in range(3):
                if flip == 0:
                    target = tile + TILES + 1 - place
                else:
                    target = 2 * TILES - tile - place
                plan.append(((link, flip, place), (partner, lax.rem(target, TILES))))
    return plan


def halo_kernel(rows_ref, strips_ref, above_ref, below_ref, ghosts_ref, send_sem, recv_sem):
    plan = halo_plan(lax.axis_index("face"), lax.axis_index("tile"))
    barrier = pltpu.get_barrier_semaphore()
    for _, target in plan:
        pl.semaphore_signal(barrier, inc=1, device_id=target, device_id_type=MESH)
    pl.semaphore_wait(barrier, len(plan))
    row_count = rows_ref.shape[0]
    copies = []
    for index, (kind, target) in enumerate(plan):
        if kind == "up":
            source, landing = rows_ref.at[0:3], below_ref
        elif kind == "down":
            source, landing = rows_ref.at[row_count - 3 : row_count], above_ref
        else:
            link, flip, place = kind
            source, landing = strips_ref.at[link], ghosts_ref.at[link, flip, place]
        copy = pltpu.make_async_remote_copy(
            src_ref=source,
            dst_ref=landing,
            send_sem=send_sem.at[index],
            recv_sem=recv_sem.at[index],
            device_id=target,
            device_id_type=MESH,
        )
        copy.start()
        copies.append(copy)
    for copy in copies:
        copy.wait()


def exchange(rows, strips, collective_id):
    row_count, col_count, channels = rows.shape
    vmem = pl.BlockSpec(memory_space=pltpu.VMEM)
    return pl.pallas_call(
        halo_kernel,
        out_shape=(
            jax.ShapeDtypeStruct((3, col_count, channels), BF16),
            jax.ShapeDtypeStruct((3, col_count, channels), BF16),
            jax.ShapeDtypeStruct((2, 2, 3) + strips.shape[1:], BF16),
        ),
        in_specs=[vmem] * 2,
        out_specs=(vmem,) * 3,
        scratch_shapes=[pltpu.SemaphoreType.DMA((14,)), pltpu.SemaphoreType.DMA((14,))],
        compiler_params=pltpu.CompilerParams(collective_id=collective_id, has_side_effects=True),
    )(rows, strips)


def halo(rows, own_match):
    def at(index):
        return index

    row_count, col_count, channels = rows.shape
    face, tile = lax.axis_index("face"), lax.axis_index("tile")
    beside_side = jnp.where(own_match[0, 0] == jnp.bitwise_xor(face, 1), 0, 1)
    west = jnp.moveaxis(rows[:, 0:3], 1, 0)
    east = jnp.moveaxis(jnp.flip(rows[:, col_count - 3 :], 1), 1, 0)
    strips = jnp.where(beside_side == 0, jnp.stack([west, east]), jnp.stack([east, west]))
    return strips, beside_side


def unpack(above, below, ghosts, own_match, beside_side):
    tile = lax.axis_index("tile")
    first, last = tile == 0, tile == TILES - 1
    above = jnp.where(first, jnp.zeros_like(above), above)
    below = jnp.where(last, jnp.zeros_like(below), below)
    turned = jnp.flip(ghosts[:, 1], 3)
    ext = []
    for kind in (ghosts[:, 0], turned):
        ext.append(jnp.concatenate([kind[:, 0, :, 5:8], kind[:, 1], kind[:, 2, :, 0:3]], axis=2))
    inside = jnp.arange(14)
    inside = ((inside >= 3) | ~first) & ((inside < 11) | ~last)
    sides = []
    for side in range(2):
        link = jnp.where(beside_side == side, 0, 1)
        pair = jnp.where(own_match[side, 2] == 1, ext[1], ext[0])
        ghost = jnp.where(link == 0, pair[0], pair[1])
        ghost = jnp.where(inside[None, :, None], ghost, jnp.zeros_like(ghost))
        sides.append(jnp.moveaxis(ghost, 0, 1))
    return above, below, sides


def coordinates():
    face, tile = lax.axis_index("face"), lax.axis_index("tile")
    core = lax.rem(tile, 2)
    z = lax.rem(lax.div(tile, 2), 8)
    x = 2 * lax.div(tile, 16) + lax.rem(face, 2)
    y = lax.div(face, 2)
    return x, y, z, core


def device_at(x, y, z, core):
    return (2 * y + lax.rem(x, 2), 16 * lax.div(x, 2) + 2 * z + core)


def reduce_kernel(
    expand_ref,
    reduce_ref,
    small_ref,
    expand_out,
    reduce_out,
    small_out,
    src,
    from_core,
    sum_core,
    from_a,
    sum_a,
    from_b,
    sum_b,
    from_z,
    gathered,
    small_core,
    small_sum,
    small_x,
    small_sum_x,
    small_y,
    small_z,
    big_send,
    big_recv,
    small_send,
    small_recv,
    scale,
):
    x, y, z, core = coordinates()
    sibling = device_at(x, y, z, 1 - core)

    def x_peer(step):
        return device_at(lax.rem(x + step, 4), y, z, core)

    def y_peer(step):
        return device_at(x, lax.rem(y + step, 4), z, core)

    def z_peer(step):
        return device_at(x, y, lax.rem(z + step, 8), core)

    place_a = x + core * (y - x)
    place_b = y + core * (x - y)

    def a_peer(step):
        new = lax.rem(place_a + step, 4)
        return device_at(new + core * (x - new), y + core * (new - y), z, core)

    def b_peer(step):
        new = lax.rem(place_b + step, 4)
        return device_at(x + core * (new - x), new + core * (y - new), z, core)

    barrier = pltpu.get_barrier_semaphore()
    peers = [sibling]
    peers += [x_peer(step) for step in range(1, 4)]
    peers += [y_peer(step) for step in range(1, 4)]
    peers += [z_peer(step) for step in range(1, 8)]
    for peer in peers:
        pl.semaphore_signal(barrier, inc=1, device_id=peer, device_id_type=MESH)

    def fill_expand(row, carry):
        block = expand_ref[pl.ds(pl.multiple_of(row * 16, 16), 16), :].astype(BF16)
        for col in range(8):
            src[0, row * 8 + col] = block[:, col * 128 : col * 128 + 128]
        return carry

    def fill_reduce(row, carry):
        block = reduce_ref[pl.ds(pl.multiple_of(row * 16, 16), 16), :].astype(BF16)
        for col in range(2):
            src[1, row * 2 + col] = block[:, col * 128 : col * 128 + 128]
        return carry

    lax.fori_loop(0, 16, fill_expand, 0)
    lax.fori_loop(0, 64, fill_reduce, 0)
    pl.semaphore_wait(barrier, len(peers))

    counters = [0, 0]

    def big(source, landing, target):
        index = counters[0]
        counters[0] += 1
        copy = pltpu.make_async_remote_copy(
            source, landing, big_send.at[index], big_recv.at[index], target, MESH
        )
        copy.start()
        return copy

    def small(source, landing, target):
        index = counters[1]
        counters[1] += 1
        copy = pltpu.make_async_remote_copy(
            source, landing, small_send.at[index], small_recv.at[index], target, MESH
        )
        copy.start()
        return copy

    def finish(copies):
        for copy in copies:
            copy.wait()

    small_copies = [small(small_ref, small_core, sibling)]
    big_copies = [big(src.at[1 - core], from_core, sibling)]
    finish(small_copies)
    small_sum[...] = small_ref[...] + small_core[...]
    small_copies = []
    for step in range(1, 4):
        chunk = lax.rem(x + step, 4)
        small_copies.append(small(small_sum.at[chunk], small_x.at[step - 1], x_peer(step)))
    finish(big_copies)

    def add_core(index, carry):
        sum_core[index] = (src[core, index].astype(F32) + from_core[index].astype(F32)).astype(BF16)
        return carry

    lax.fori_loop(0, 128, add_core, 0, unroll=8)
    big_copies = []
    for step in range(1, 4):
        chunk = lax.rem(place_a + step, 4)
        big_copies.append(
            big(sum_core.at[pl.ds(chunk * 32, 32)], from_a.at[step - 1], a_peer(step))
        )
    finish(small_copies)
    small_sum_x[...] = small_sum[x] + small_x[0] + small_x[1] + small_x[2]
    small_copies = []
    for step in range(1, 4):
        chunk = lax.rem(y + step, 4)
        small_copies.append(small(small_sum_x.at[chunk], small_y.at[step - 1], y_peer(step)))
    finish(big_copies)

    def add_a(index, carry):
        total = sum_core[place_a * 32 + index].astype(F32)
        for step in range(3):
            total = total + from_a[step, index].astype(F32)
        sum_a[index] = total.astype(BF16)
        return carry

    lax.fori_loop(0, 32, add_a, 0, unroll=8)
    big_copies = []
    for step in range(1, 4):
        chunk = lax.rem(place_b + step, 4)
        big_copies.append(big(sum_a.at[pl.ds(chunk * 8, 8)], from_b.at[step - 1], b_peer(step)))
    finish(small_copies)
    small_z[z] = small_sum_x[y] + small_y[0] + small_y[1] + small_y[2]
    small_copies = []
    for step in range(1, 8):
        small_copies.append(small(small_z.at[z], small_z.at[z], z_peer(step)))
    finish(big_copies)

    def add_b(index, carry):
        total = sum_a[place_b * 8 + index].astype(F32)
        for step in range(3):
            total = total + from_b[step, index].astype(F32)
        sum_b[index] = total.astype(BF16)
        return carry

    lax.fori_loop(0, 8, add_b, 0, unroll=8)
    big_copies = []
    for step in range(1, 8):
        big_copies.append(big(sum_b.at[lax.rem(z + step, 8)], from_z.at[step - 1], z_peer(step)))
    finish(small_copies)
    total = small_z[0]
    for step in range(1, 8):
        total = total + small_z[step]
    small_out[x, y] = total * scale
    small_copies = []
    for step in range(1, 4):
        small_copies.append(small(small_out.at[x, y], small_out.at[x, y], y_peer(step)))
    finish(big_copies)
    total = sum_b[z].astype(F32)
    for step in range(7):
        total = total + from_z[step].astype(F32)
    own = place_a * 32 + place_b * 8 + z
    gathered[core, own] = total.astype(BF16)
    big_copies = []
    for step in range(1, 8):
        big_copies.append(big(gathered.at[core, own], gathered.at[core, own], z_peer(step)))
    finish(small_copies)
    small_copies = []
    for step in range(1, 4):
        small_copies.append(small(small_out.at[x], small_out.at[x], x_peer(step)))
    finish(big_copies)
    block = pl.ds(place_a * 32 + place_b * 8, 8)
    big_copies = []
    for step in range(1, 4):
        big_copies.append(big(gathered.at[core, block], gathered.at[core, block], b_peer(step)))
    finish(big_copies)
    wide = pl.ds(place_a * 32, 32)
    big_copies = []
    for step in range(1, 4):
        big_copies.append(big(gathered.at[core, wide], gathered.at[core, wide], a_peer(step)))
    finish(big_copies)
    big_copies = [big(gathered.at[core], gathered.at[core], sibling)]
    finish(small_copies)
    finish(big_copies)

    def empty_expand(row, carry):
        rows = pl.ds(pl.multiple_of(row * 16, 16), 16)
        for col in range(8):
            expand_out[rows, col * 128 : col * 128 + 128] = (
                gathered[0, row * 8 + col].astype(F32) * scale
            )
        return carry

    def empty_reduce(row, carry):
        rows = pl.ds(pl.multiple_of(row * 16, 16), 16)
        for col in range(2):
            reduce_out[rows, col * 128 : col * 128 + 128] = (
                gathered[1, row * 2 + col].astype(F32) * scale
            )
        return carry

    lax.fori_loop(0, 16, empty_expand, 0)
    lax.fori_loop(0, 64, empty_reduce, 0)


def reduce_all(grad_expand, grad_reduce, small, scale):
    vmem = pl.BlockSpec(memory_space=pltpu.VMEM)
    tile = (16, 128)
    return pl.pallas_call(
        functools.partial(reduce_kernel, scale=scale),
        out_shape=(
            jax.ShapeDtypeStruct(grad_expand.shape, F32),
            jax.ShapeDtypeStruct(grad_reduce.shape, F32),
            jax.ShapeDtypeStruct(small.shape, F32),
        ),
        in_specs=[vmem] * 3,
        out_specs=(vmem,) * 3,
        scratch_shapes=[
            pltpu.VMEM((2, 128) + tile, BF16),
            pltpu.VMEM((128,) + tile, BF16),
            pltpu.VMEM((128,) + tile, BF16),
            pltpu.VMEM((3, 32) + tile, BF16),
            pltpu.VMEM((32,) + tile, BF16),
            pltpu.VMEM((3, 8) + tile, BF16),
            pltpu.VMEM((8,) + tile, BF16),
            pltpu.VMEM((7,) + tile, BF16),
            pltpu.VMEM((2, 128) + tile, BF16),
            pltpu.VMEM((4, 4, 8, 128), F32),
            pltpu.VMEM((4, 4, 8, 128), F32),
            pltpu.VMEM((3, 4, 8, 128), F32),
            pltpu.VMEM((4, 8, 128), F32),
            pltpu.VMEM((3, 8, 128), F32),
            pltpu.VMEM((8, 8, 128), F32),
            pltpu.SemaphoreType.DMA((28,)),
            pltpu.SemaphoreType.DMA((28,)),
            pltpu.SemaphoreType.DMA((20,)),
            pltpu.SemaphoreType.DMA((20,)),
        ],
        compiler_params=pltpu.CompilerParams(collective_id=2, has_side_effects=True),
    )(grad_expand, grad_reduce, small)


def gelu_pair(preact):
    argument = ROOT_COEF * (preact + CUBIC_COEF * preact * preact * preact)
    tanhed = jnp.tanh(argument)
    gelu_value = 0.5 * preact * (1.0 + tanhed)
    gelu_slope = 0.5 * (1.0 + tanhed) + 0.5 * preact * (1.0 - tanhed * tanhed) * ROOT_COEF * (
        1.0 + 3.0 * CUBIC_COEF * preact * preact
    )
    return (gelu_value, gelu_slope)


def contract_rows(left_side, right_side):
    return lax.dot_general(
        left_side, right_side, (((0,), (0,)), ((), ())), preferred_element_type=F32
    )


def contract_cols(left_side, right_side):
    return lax.dot_general(
        left_side, right_side, (((1,), (1,)), ((), ())), preferred_element_type=F32
    )


def shards(
    fields,
    cotangent,
    edge_match,
    depth_kernel,
    depth_bias,
    norm_gain,
    norm_bias,
    expand_weight,
    expand_bias,
    reduce_weight,
    reduce_bias,
    layer_scale,
):
    band = fields[0]
    row_count, col_count, channels = band.shape
    cells = row_count * col_count
    own_match = lax.dynamic_index_in_dim(edge_match, lax.axis_index("face"), 0, keepdims=False)
    strips, beside_side = halo(band, own_match)
    above, below, (west, east) = unpack(*exchange(band, strips, 0), own_match, beside_side)
    tall = jnp.concatenate([above, band, below], axis=0)
    padded = jnp.concatenate([jnp.flip(west, 1), tall, east], axis=1).astype(F32)
    kernel = depth_kernel.astype(F32)

    convolved = jnp.zeros((row_count, col_count, channels), F32) + depth_bias
    for row_off in range(7):
        for col_off in range(7):
            convolved = (
                convolved
                + kernel[row_off, col_off]
                * padded[row_off : row_off + row_count, col_off : col_off + col_count]
            )
    average = jnp.mean(convolved, axis=-1, keepdims=True)
    centred = convolved - average
    inverse = lax.rsqrt(jnp.mean(centred * centred, axis=-1, keepdims=True) + EPSILON)
    standard = centred * inverse
    normed = (standard * norm_gain + norm_bias).astype(BF16).reshape(cells, channels)
    preact = jnp.dot(normed, expand_weight, preferred_element_type=F32) + expand_bias
    gelu_value, gelu_slope = gelu_pair(preact)
    activated = gelu_value.astype(BF16)
    branch = jnp.dot(activated, reduce_weight, preferred_element_type=F32) + reduce_bias
    residual = band.reshape(cells, channels).astype(F32)
    result = (residual + layer_scale * branch).astype(BF16).reshape(band.shape)
    upstream = cotangent[0].reshape(cells, channels).astype(F32)
    grad_branch = (upstream * layer_scale).astype(BF16)
    grad_pre = (contract_cols(grad_branch, reduce_weight) * gelu_slope).astype(BF16)
    grad_normed = contract_cols(grad_pre, expand_weight).reshape(row_count, col_count, channels)
    scaled = grad_normed * norm_gain
    grad_conv = (
        scaled
        - jnp.mean(scaled, axis=-1, keepdims=True)
        - standard * jnp.mean(scaled * standard, axis=-1, keepdims=True)
    ) * inverse

    grad_rows = grad_conv.astype(BF16)
    strips, _ = halo(grad_rows, own_match)
    above, below, ghosts = unpack(*exchange(grad_rows, strips, 1), own_match, beside_side)
    tall = jnp.concatenate([above.astype(F32), grad_conv, below.astype(F32)], axis=0)
    tall = jnp.pad(tall, ((0, 0), (3, 3), (0, 0)))
    interior = cotangent[0].astype(F32)
    kernel_terms = []
    for row_off in range(7):
        for col_off in range(7):
            interior = (
                interior
                + kernel[row_off, col_off]
                * tall[6 - row_off : 6 - row_off + row_count, 6 - col_off : 6 - col_off + col_count]
            )
            kernel_terms.append(
                jnp.sum(
                    grad_conv
                    * padded[row_off : row_off + row_count, col_off : col_off + col_count],
                    axis=(0, 1),
                )
            )
    for side in range(2):
        taps = jnp.where(own_match[side, 2] == 1, jnp.flip(kernel, 0), kernel)
        taps = jnp.where(own_match[side, 1] == 1, taps[:, 4:7], jnp.flip(taps[:, 0:3], 1))
        ghost = ghosts[side].astype(F32)
        columns = []
        for depth in range(3):
            total = jnp.zeros((row_count, channels), F32)
            for other in range(3 - depth):
                for row_off in range(7):
                    total = (
                        total
                        + taps[row_off, depth + other]
                        * ghost[6 - row_off : 6 - row_off + row_count, other]
                    )
            columns.append(total)
        if side == 0:
            interior = interior.at[:, 0:3].add(jnp.stack(columns, 1))
        else:
            interior = interior.at[:, col_count - 3 :].add(jnp.stack(columns[::-1], 1))
    grad_fields = interior.astype(BF16)

    vectors = jnp.stack(
        [
            jnp.sum(grad_conv, axis=(0, 1)),
            jnp.sum(grad_normed * standard, axis=(0, 1)),
            jnp.sum(grad_normed, axis=(0, 1)),
            jnp.sum(upstream, axis=0) * layer_scale,
            jnp.sum(upstream * branch, axis=0),
        ]
    )
    grad_expand_bias = jnp.sum(grad_pre.astype(F32), axis=0)
    small = jnp.concatenate(
        [
            jnp.stack(kernel_terms).reshape(-1),
            grad_expand_bias,
            vectors.reshape(-1),
            jnp.zeros((6 * 256,), F32),
        ]
    ).reshape(4, 4, 8, 128)
    grad_expand = contract_rows(normed, grad_pre)
    grad_reduce = contract_rows(activated, grad_branch)
    scale = 1.0 / math.sqrt(FACES * TILES * cells)
    grad_expand, grad_reduce, small = reduce_all(grad_expand, grad_reduce, small, scale)
    small = small.reshape(-1)
    return (
        result[None],
        grad_fields[None],
        small[: 49 * 256].reshape(7, 7, 256),
        grad_expand,
        grad_reduce,
        small[49 * 256 : 53 * 256],
        small[53 * 256 : 58 * 256].reshape(5, 256),
    )


def solution(mesh):
    return jax.shard_map(
        shards,
        mesh=mesh,
        in_specs=(P("face", "tile", None, None),) * 2 + (P(),) * 10,
        out_specs=(P("face", "tile", None, None),) * 2 + (P(),) * 5,
        check_vma=False,
    )
```

```python
import functools
import math

import jax
import jax.numpy as jnp
from jax import lax
from jax.experimental import pallas as pl
from jax.experimental.pallas import tpu as pltpu
from jax.sharding import PartitionSpec as P

EPSILON = 1e-06
ROOT_COEF = 0.7978845608028654
CUBIC_COEF = 0.044715
MESH = pl.DeviceIdType.MESH
FACES = 8
TILES = 32
ROWS = 8
COLS = 128
CH = 256
HID = 1024
F32 = jnp.float32
BF16 = jnp.bfloat16
OWN_PAIRS = [(i, a) for i in range(ROWS) for a in range(7) if 3 <= i + a <= 10]
RIM_PAIRS = [(i, a) for i in range(ROWS) for a in range(7) if not 3 <= i + a <= 10]


def halo_plan(face, tile):
    beside = face + 1 - 2 * lax.rem(face, 2)
    across = lax.rem(face + 4, FACES)
    plan = [
        ("up", (face, lax.rem(tile + TILES - 1, TILES))),
        ("down", (face, lax.rem(tile + 1, TILES))),
    ]
    for link, partner in enumerate((beside, across)):
        for flip in range(2):
            for place in range(3):
                if flip == 0:
                    target = tile + TILES + 1 - place
                else:
                    target = 2 * TILES - tile - place
                plan.append(((link, flip, place), (partner, lax.rem(target, TILES))))
    return plan


def device_at(x, y, z, core):
    return (2 * y + lax.rem(x, 2), 16 * lax.div(x, 2) + 2 * z + core)


def pick(flag, if_one, if_zero):
    return jnp.where(jnp.broadcast_to(flag, if_one.shape) == 1, if_one, if_zero)


def dot_nn(left, right):
    return lax.dot_general(left, right, (((1,), (0,)), ((), ())), preferred_element_type=F32)


def dot_nt(left, right):
    return lax.dot_general(left, right, (((1,), (1,)), ((), ())), preferred_element_type=F32)


def fold(block):
    return jnp.sum(block.reshape(16, 8, block.shape[1]), axis=0)


def conv_chunk(shifted, taps, flipped, out, chunk, pairs, start):
    cols = pl.ds(pl.multiple_of(chunk * 8, 8), 8)
    for half in range(2):
        lanes = slice(half * 128, half * 128 + 128)
        acc = {}
        for i in sorted({i for i, _ in pairs}):
            acc[i] = out[i, cols, lanes] if start is None else start[:, lanes]
        for b in range(7):
            rows = {r: shifted[b, r, cols, lanes] for r in sorted({i + a for i, a in pairs})}
            for a in sorted({a for _, a in pairs}):
                tap = taps[48 - a * 7 - b if flipped else a * 7 + b, :, lanes]
                for i in sorted({i for i, a2 in pairs if a2 == a}):
                    acc[i] = acc[i] + tap * rows[i + a]
        for i, value in acc.items():
            out[i, cols, lanes] = value


def block_kernel(
    edge_ref,
    fields_ref,
    cot_ref,
    taps_ref,
    depth_bias_ref,
    gain_ref,
    norm_bias_ref,
    w1_ref,
    b1_ref,
    w2_ref,
    b2_ref,
    scale_ref,
    result_ref,
    gfields_ref,
    gkernel_ref,
    gexpand_ref,
    greduce_ref,
    gbias_ref,
    gvectors_ref,
    taps,
    wide,
    shifted,
    shifted_g,
    strip_f,
    strips,
    above,
    below,
    ghosts,
    ghost_f,
    rows_g,
    strips_g,
    above_g,
    below_g,
    ghosts_g,
    conv,
    standard,
    inverse,
    normed,
    normed_t,
    cot_branch_t,
    grad_hidden,
    active,
    grad_pre,
    bias_sum,
    vector_sum,
    src,
    from_core,
    sum_core,
    from_a,
    sum_a,
    from_b,
    sum_b,
    from_z,
    gathered,
    small_in,
    small_core,
    small_sum,
    small_x,
    small_sum_x,
    small_y,
    small_z,
    small_out,
    halo_send,
    halo_recv,
    grad_send,
    grad_recv,
    big_send,
    big_recv,
    small_send,
    small_recv,
    factor,
):
    face, tile = lax.axis_index("face"), lax.axis_index("tile")
    core = lax.rem(tile, 2)
    z = lax.rem(lax.div(tile, 2), 8)
    x = 2 * lax.div(tile, 16) + lax.rem(face, 2)
    y = lax.div(face, 2)
    sibling = device_at(x, y, z, 1 - core)

    def x_peer(step):
        return device_at(lax.rem(x + step, 4), y, z, core)

    def y_peer(step):
        return device_at(x, lax.rem(y + step, 4), z, core)

    def z_peer(step):
        return device_at(x, y, lax.rem(z + step, 8), core)

    place_a = x + core * (y - x)
    place_b = y + core * (x - y)

    def a_peer(step):
        new = lax.rem(place_a + step, 4)
        return device_at(new + core * (x - new), y + core * (new - y), z, core)

    def b_peer(step):
        new = lax.rem(place_b + step, 4)
        return device_at(x + core * (new - x), new + core * (y - new), z, core)

    plan = halo_plan(face, tile)
    barrier = pltpu.get_barrier_semaphore()
    peers = [target for _, target in plan]
    peers += [sibling]
    peers += [x_peer(step) for step in range(1, 4)]
    peers += [y_peer(step) for step in range(1, 4)]
    peers += [z_peer(step) for step in range(1, 8)]
    for peer in peers:
        pl.semaphore_signal(barrier, inc=1, device_id=peer, device_id_type=MESH)

    first = jnp.where(tile == 0, 1, 0)
    last = jnp.where(tile == TILES - 1, 1, 0)
    beside = face + 1 - 2 * lax.rem(face, 2)
    beside_side = jnp.where(edge_ref[face * 6] == beside, 0, 1)

    def make_strips(target):
        for row in range(ROWS):
            for depth in range(3):
                for side, col in ((0, 8 + depth), (1, 135 - depth)):
                    piece = wide[3 + row, col : col + 1, :]
                    strip_f[side, 0, depth, row : row + 1, :] = piece
                    strip_f[side, 1, depth, 7 - row : 8 - row, :] = piece
        for flip in range(2):
            for depth in range(3):
                west, east = strip_f[0, flip, depth], strip_f[1, flip, depth]
                target[0, flip, depth] = pick(beside_side, east, west).astype(BF16)
                target[1, flip, depth] = pick(beside_side, west, east).astype(BF16)

    def start_halo(rows, strip, to_above, to_below, to_ghosts, send, recv):
        copies = []
        for index, (kind, target) in enumerate(plan):
            if kind == "up":
                source, landing = rows.at[0:3], to_below
            elif kind == "down":
                source, landing = rows.at[ROWS - 3 : ROWS], to_above
            else:
                link, flip, place = kind
                source, landing = strip.at[link, flip], to_ghosts.at[link, flip, place]
            copy = pltpu.make_async_remote_copy(
                source, landing, send.at[index], recv.at[index], target, MESH
            )
            copy.start()
            copies.append(copy)
        return copies

    def take_ghosts(source):
        for side in range(2):
            reverse = edge_ref[face * 6 + side * 3 + 2]
            other = beside_side if side == 0 else 1 - beside_side
            for place in range(3):
                for depth in range(3):
                    values = [
                        pick(
                            other,
                            source[1, flip, place, depth].astype(F32),
                            source[0, flip, place, depth].astype(F32),
                        )
                        for flip in range(2)
                    ]
                    value = pick(reverse, values[1], values[0])
                    if place == 0:
                        value = pick(first, jnp.zeros_like(value), value)
                    if place == 2:
                        value = pick(last, jnp.zeros_like(value), value)
                    ghost_f[side, depth, place * 8 : place * 8 + 8, :] = value

    def take_rows(source_above, source_below):
        for row in range(3):
            value = source_above[row].astype(F32)
            wide[row, 8:136, :] = pick(first, jnp.zeros_like(value), value)
            value = source_below[row].astype(F32)
            wide[11 + row, 8:136, :] = pick(last, jnp.zeros_like(value), value)

    def shift_row(target, row):
        for b in range(7):
            target[b, row] = wide[row, 5 + b : 133 + b, :]

    for a in range(7):
        block = taps_ref[a].astype(F32)
        for b in range(7):
            taps[a * 7 + b] = jnp.broadcast_to(block[b : b + 1, :], (8, CH))
    edge_zero = jnp.zeros((8, CH), F32)

    def load_row(row, carry):
        wide[3 + row, 0:8, :] = edge_zero
        wide[3 + row, 136:144, :] = edge_zero
        wide[3 + row, 8:136, :] = fields_ref[row].astype(F32)
        return carry

    lax.fori_loop(0, ROWS, load_row, 0)
    make_strips(strips)
    vector_sum[...] = jnp.zeros_like(vector_sum)
    bias_sum[...] = jnp.zeros_like(bias_sum)

    def own_shift(row, carry):
        shift_row(shifted, 3 + row)
        return carry

    lax.fori_loop(0, ROWS, own_shift, 0)
    pl.semaphore_wait(barrier, len(peers))
    halo = start_halo(fields_ref, strips, above, below, ghosts, halo_send, halo_recv)

    def cot_row(row, carry):
        cells = pl.ds(pl.multiple_of(row * COLS, COLS), COLS)
        upstream = cot_ref[row].astype(F32)
        scaled = upstream * scale_ref[...]
        branch_grad = scaled.astype(BF16)
        cot_branch_t[:, cells] = jnp.transpose(scaled).astype(BF16)
        vector_sum[3] = vector_sum[3] + fold(upstream)
        for part in range(4):
            hidden = slice(part * 256, part * 256 + 256)
            grad_hidden[cells, hidden] = dot_nt(branch_grad, w2_ref[hidden, :])
        return carry

    lax.fori_loop(0, ROWS, cot_row, 0)
    start = jnp.broadcast_to(depth_bias_ref[...], (8, CH))

    def own_conv(chunk, carry):
        conv_chunk(shifted, taps, False, conv, chunk, OWN_PAIRS, start)
        return carry

    lax.fori_loop(1, 15, own_conv, 0)
    for copy in halo:
        copy.wait()

    take_ghosts(ghosts)
    take_rows(above, below)
    for row in range(14):
        for depth in range(3):
            wide[row, 7 - depth : 8 - depth, :] = ghost_f[0, depth, row + 5 : row + 6, :]
            wide[row, 136 + depth : 137 + depth, :] = ghost_f[1, depth, row + 5 : row + 6, :]

    def rim_shift(row, carry):
        shift_row(shifted, row)
        shift_row(shifted, 11 + row)
        return carry

    lax.fori_loop(0, 3, rim_shift, 0)

    def edge_shift(row, carry):
        for b in range(7):
            shifted[b, 3 + row, 0:8, :] = wide[3 + row, 5 + b : 13 + b, :]
            shifted[b, 3 + row, 120:128, :] = wide[3 + row, 125 + b : 133 + b, :]
        return carry

    lax.fori_loop(0, ROWS, edge_shift, 0)

    def rim_conv(chunk, carry):
        conv_chunk(shifted, taps, False, conv, chunk, RIM_PAIRS, None)
        return carry

    lax.fori_loop(1, 15, rim_conv, 0)

    def edge_conv(index, carry):
        conv_chunk(shifted, taps, False, conv, index * 15, OWN_PAIRS + RIM_PAIRS, start)
        return carry

    lax.fori_loop(0, 2, edge_conv, 0)

    def norm_row(row, carry):
        cells = pl.ds(pl.multiple_of(row * COLS, COLS), COLS)
        value = conv[row]
        centred = value - jnp.sum(value, axis=1, keepdims=True) * (1.0 / CH)
        variance = jnp.sum(centred * centred, axis=1, keepdims=True) * (1.0 / CH)
        inv = lax.rsqrt(variance + EPSILON)
        std = centred * inv
        standard[row] = std
        inverse[row] = inv
        scaled = std * gain_ref[...] + norm_bias_ref[...]
        block = scaled.astype(BF16)
        normed[cells, :] = block
        normed_t[:, cells] = jnp.transpose(scaled).astype(BF16)
        for part in range(4):
            hidden = slice(part * 256, part * 256 + 256)
            pre = dot_nn(block, w1_ref[:, hidden]) + b1_ref[:, hidden]
            square = pre * pre
            tanhed = jnp.tanh(pre * (ROOT_COEF + (ROOT_COEF * CUBIC_COEF) * square))
            half_pre = 0.5 * pre
            plus = 1.0 + tanhed
            active[cells, hidden] = (half_pre * plus).astype(BF16)
            slope = 0.5 * plus + (half_pre * (1.0 - tanhed * tanhed)) * (
                ROOT_COEF + (3.0 * ROOT_COEF * CUBIC_COEF) * square
            )
            grad = (grad_hidden[cells, hidden] * slope).astype(BF16)
            grad_pre[cells, hidden] = grad
            bias_sum[:, hidden] = bias_sum[:, hidden] + fold(grad.astype(F32))
        return carry

    lax.fori_loop(0, ROWS, norm_row, 0)

    def expand_part(part, carry):
        hidden = pl.ds(pl.multiple_of(part * 256, 256), 256)
        block = dot_nn(normed_t[...], grad_pre[:, hidden]).astype(BF16)
        for row in range(16):
            for col in range(2):
                src[0, row * 8 + part * 2 + col] = block[
                    row * 16 : row * 16 + 16, col * 128 : col * 128 + 128
                ]
        return carry

    def reduce_part(part, carry):
        hidden = pl.ds(pl.multiple_of(part * 256, 256), 256)
        block = jnp.transpose(dot_nn(cot_branch_t[...], active[:, hidden])).astype(BF16)
        for row in range(16):
            for col in range(2):
                src[1, part * 32 + row * 2 + col] = block[
                    row * 16 : row * 16 + 16, col * 128 : col * 128 + 128
                ]
        return carry

    lax.fori_loop(0, 4, expand_part, 0)
    lax.fori_loop(0, 4, reduce_part, 0)

    counters = [0, 0]

    def big(source, landing, target):
        index = counters[0]
        counters[0] += 1
        copy = pltpu.make_async_remote_copy(
            source, landing, big_send.at[index], big_recv.at[index], target, MESH
        )
        copy.start()
        return copy

    def small(source, landing, target):
        index = counters[1]
        counters[1] += 1
        copy = pltpu.make_async_remote_copy(
            source, landing, small_send.at[index], small_recv.at[index], target, MESH
        )
        copy.start()
        return copy

    def finish(copies):
        for copy in copies:
            copy.wait()

    big_copies = [big(src.at[1 - core], from_core, sibling)]

    def grad_row(row, carry):
        cells = pl.ds(pl.multiple_of(row * COLS, COLS), COLS)
        grad_normed = dot_nt(grad_pre[cells, :], w1_ref[...])
        std = standard[row]
        scaled = grad_normed * gain_ref[...]
        mean = jnp.sum(scaled, axis=1, keepdims=True) * (1.0 / CH)
        slant = jnp.sum(scaled * std, axis=1, keepdims=True) * (1.0 / CH)
        grad = (scaled - mean - std * slant) * inverse[row]
        conv[row] = grad
        wide[3 + row, 0:8, :] = edge_zero
        wide[3 + row, 136:144, :] = edge_zero
        wide[3 + row, 8:136, :] = grad
        rows_g[row] = grad.astype(BF16)
        vector_sum[0] = vector_sum[0] + fold(grad)
        vector_sum[1] = vector_sum[1] + fold(grad_normed * std)
        vector_sum[2] = vector_sum[2] + fold(grad_normed)
        return carry

    lax.fori_loop(0, ROWS, grad_row, 0)
    make_strips(strips_g)
    halo = start_halo(rows_g, strips_g, above_g, below_g, ghosts_g, grad_send, grad_recv)

    finish(big_copies)

    def add_core(index, carry):
        sum_core[index] = (src[core, index].astype(F32) + from_core[index].astype(F32)).astype(BF16)
        return carry

    lax.fori_loop(0, 128, add_core, 0, unroll=8)
    big_copies = []
    for step in range(1, 4):
        chunk = lax.rem(place_a + step, 4)
        big_copies.append(
            big(sum_core.at[pl.ds(chunk * 32, 32)], from_a.at[step - 1], a_peer(step))
        )

    def result_row(row, carry):
        cells = pl.ds(pl.multiple_of(row * COLS, COLS), COLS)
        branch = dot_nn(active[cells, :], w2_ref[...]) + b2_ref[...]
        result_ref[row] = (fields_ref[row].astype(F32) + scale_ref[...] * branch).astype(BF16)
        vector_sum[4] = vector_sum[4] + fold(cot_ref[row].astype(F32) * branch)
        return carry

    lax.fori_loop(0, ROWS, result_row, 0)

    small_in[...] = jnp.zeros_like(small_in)
    for b in range(7):

        def tap_sums(chunk, carry):
            cols = pl.ds(pl.multiple_of(chunk * 8, 8), 8)
            sums = list(carry)
            for half in range(2):
                lanes = slice(half * 128, half * 128 + 128)
                grads = [conv[i, cols, lanes] for i in range(ROWS)]
                for r in range(14):
                    value = shifted[b, r, cols, lanes]
                    for a in range(7):
                        if 0 <= r - a < ROWS:
                            sums[a * 2 + half] = sums[a * 2 + half] + grads[r - a] * value
            return tuple(sums)

        sums = lax.fori_loop(0, 16, tap_sums, tuple(jnp.zeros((8, 128), F32) for _ in range(14)))
        for index, value in enumerate(sums):
            small_in[index, b : b + 1, :] = jnp.sum(value, axis=0, keepdims=True)
    for part in range(8):
        small_in[part, 7:8, :] = jnp.sum(
            bias_sum[:, part * 128 : part * 128 + 128], axis=0, keepdims=True
        )
    for row in range(5):
        total = jnp.sum(vector_sum[row], axis=0, keepdims=True)
        if row == 3:
            total = total * scale_ref[...]
        for half in range(2):
            small_in[14 + half, row : row + 1, :] = total[:, half * 128 : half * 128 + 128]
    small_copies = [small(small_in, small_core, sibling)]

    finish(big_copies)

    def add_a(index, carry):
        total = sum_core[place_a * 32 + index].astype(F32)
        for step in range(3):
            total = total + from_a[step, index].astype(F32)
        sum_a[index] = total.astype(BF16)
        return carry

    lax.fori_loop(0, 32, add_a, 0, unroll=8)
    big_copies = []
    for step in range(1, 4):
        chunk = lax.rem(place_b + step, 4)
        big_copies.append(big(sum_a.at[pl.ds(chunk * 8, 8)], from_b.at[step - 1], b_peer(step)))

    def own_shift_g(row, carry):
        shift_row(shifted_g, 3 + row)
        return carry

    lax.fori_loop(0, ROWS, own_shift_g, 0)
    finish(small_copies)
    small_sum[...] = small_in[...] + small_core[...]
    small_copies = []
    for step in range(1, 4):
        chunk = lax.rem(x + step, 4)
        small_copies.append(
            small(small_sum.at[pl.ds(chunk * 4, 4)], small_x.at[step - 1], x_peer(step))
        )
    finish(big_copies)

    def add_b(index, carry):
        total = sum_a[place_b * 8 + index].astype(F32)
        for step in range(3):
            total = total + from_b[step, index].astype(F32)
        sum_b[index] = total.astype(BF16)
        return carry

    lax.fori_loop(0, 8, add_b, 0, unroll=8)
    big_copies = []
    for step in range(1, 8):
        big_copies.append(big(sum_b.at[lax.rem(z + step, 8)], from_z.at[step - 1], z_peer(step)))

    def own_conv_g(chunk, carry):
        conv_chunk(shifted_g, taps, True, conv, chunk, OWN_PAIRS, edge_zero)
        return carry

    lax.fori_loop(0, 8, own_conv_g, 0)

    finish(small_copies)
    small_sum_x[...] = small_sum[pl.ds(x * 4, 4)] + small_x[0] + small_x[1] + small_x[2]
    small_copies = []
    for step in range(1, 4):
        chunk = lax.rem(y + step, 4)
        small_copies.append(small(small_sum_x.at[chunk], small_y.at[step - 1], y_peer(step)))
    finish(big_copies)
    total = sum_b[z].astype(F32)
    for step in range(7):
        total = total + from_z[step].astype(F32)
    own = place_a * 32 + place_b * 8 + z
    gathered[core, own] = total.astype(BF16)
    big_copies = []
    for step in range(1, 8):
        big_copies.append(big(gathered.at[core, own], gathered.at[core, own], z_peer(step)))

    lax.fori_loop(8, 16, own_conv_g, 0)

    finish(small_copies)
    small_z[z] = small_sum_x[y] + small_y[0] + small_y[1] + small_y[2]
    small_copies = []
    for step in range(1, 8):
        small_copies.append(small(small_z.at[z], small_z.at[z], z_peer(step)))
    finish(big_copies)
    block = pl.ds(place_a * 32 + place_b * 8, 8)
    big_copies = []
    for step in range(1, 4):
        big_copies.append(big(gathered.at[core, block], gathered.at[core, block], b_peer(step)))

    for copy in halo:
        copy.wait()
    take_ghosts(ghosts_g)
    take_rows(above_g, below_g)
    for row in range(3):
        for side_row in (row, 11 + row):
            wide[side_row, 0:8, :] = edge_zero
            wide[side_row, 136:144, :] = edge_zero

    def rim_shift_g(row, carry):
        shift_row(shifted_g, row)
        shift_row(shifted_g, 11 + row)
        return carry

    lax.fori_loop(0, 3, rim_shift_g, 0)
    finish(small_copies)
    total = small_z[0]
    for step in range(1, 8):
        total = total + small_z[step]
    mine = x * 4 + y
    small_out[mine] = total * factor
    small_copies = []
    for step in range(1, 4):
        small_copies.append(small(small_out.at[mine], small_out.at[mine], y_peer(step)))
    finish(big_copies)
    wide_block = pl.ds(place_a * 32, 32)
    big_copies = []
    for step in range(1, 4):
        big_copies.append(
            big(gathered.at[core, wide_block], gathered.at[core, wide_block], a_peer(step))
        )

    def rim_conv_g(chunk, carry):
        conv_chunk(shifted_g, taps, True, conv, chunk, RIM_PAIRS, None)
        return carry

    lax.fori_loop(0, 16, rim_conv_g, 0)
    for side in range(2):
        partner_side = edge_ref[face * 6 + side * 3 + 1]
        reverse = edge_ref[face * 6 + side * 3 + 2]
        totals = [jnp.zeros((8, CH), F32) for _ in range(3)]
        for a in range(7):
            weights = []
            for offset in range(1, 4):
                weights.append(
                    pick(
                        partner_side,
                        pick(reverse, taps[(6 - a) * 7 + 3 + offset], taps[a * 7 + 3 + offset]),
                        pick(reverse, taps[(6 - a) * 7 + 3 - offset], taps[a * 7 + 3 - offset]),
                    )
                )
            for other in range(3):
                value = ghost_f[side, other, 11 - a : 19 - a, :]
                for depth in range(3 - other):
                    totals[depth] = totals[depth] + weights[depth + other] * value
        for depth in range(3):
            strip_f[side, 0, depth] = totals[depth]
            col = depth if side == 0 else COLS - 1 - depth
            for row in range(ROWS):
                conv[row, col : col + 1, :] = (
                    conv[row, col : col + 1, :] + strip_f[side, 0, depth, row : row + 1, :]
                )
    finish(small_copies)
    mine_x = pl.ds(x * 4, 4)
    small_copies = []
    for step in range(1, 4):
        small_copies.append(small(small_out.at[mine_x], small_out.at[mine_x], x_peer(step)))

    def fields_row(row, carry):
        gfields_ref[row] = (conv[row] + cot_ref[row].astype(F32)).astype(BF16)
        return carry

    lax.fori_loop(0, ROWS, fields_row, 0)
    finish(big_copies)
    big_copies = [big(gathered.at[core], gathered.at[core], sibling)]
    finish(small_copies)
    for a in range(7):
        for half in range(2):
            gkernel_ref[a, :, half * 128 : half * 128 + 128] = small_out[2 * a + half, 0:7, :]
    for part in range(8):
        gbias_ref[part : part + 1, :] = small_out[part, 7:8, :]
    for half in range(2):
        gvectors_ref[:, half * 128 : half * 128 + 128] = small_out[14 + half, 0:5, :]
    finish(big_copies)

    def empty_expand(row, carry):
        rows = pl.ds(pl.multiple_of(row * 16, 16), 16)
        for col in range(8):
            gexpand_ref[rows, col * 128 : col * 128 + 128] = (
                gathered[0, row * 8 + col].astype(F32) * factor
            )
        return carry

    def empty_reduce(row, carry):
        rows = pl.ds(pl.multiple_of(row * 16, 16), 16)
        for col in range(2):
            greduce_ref[rows, col * 128 : col * 128 + 128] = (
                gathered[1, row * 2 + col].astype(F32) * factor
            )
        return carry

    lax.fori_loop(0, 16, empty_expand, 0)
    lax.fori_loop(0, 64, empty_reduce, 0, unroll=4)


def shards(
    fields,
    cotangent,
    edge_match,
    depth_kernel,
    depth_bias,
    norm_gain,
    norm_bias,
    expand_weight,
    expand_bias,
    reduce_weight,
    reduce_bias,
    layer_scale,
):
    vmem = pl.BlockSpec(memory_space=pltpu.VMEM)
    smem = pl.BlockSpec(memory_space=pltpu.SMEM)
    tile = (16, 128)
    cells = ROWS * COLS
    factor = 1.0 / math.sqrt(FACES * TILES * cells)
    halo_scratch = [
        pltpu.VMEM((2, 2, 3, 8, CH), BF16),
        pltpu.VMEM((3, COLS, CH), BF16),
        pltpu.VMEM((3, COLS, CH), BF16),
        pltpu.VMEM((2, 2, 3, 3, 8, CH), BF16),
    ]
    result, gfields, gkernel, gexpand, greduce, gbias, gvectors = pl.pallas_call(
        functools.partial(block_kernel, factor=factor),
        out_shape=(
            jax.ShapeDtypeStruct((ROWS, COLS, CH), BF16),
            jax.ShapeDtypeStruct((ROWS, COLS, CH), BF16),
            jax.ShapeDtypeStruct((7, 7, CH), F32),
            jax.ShapeDtypeStruct((CH, HID), F32),
            jax.ShapeDtypeStruct((HID, CH), F32),
            jax.ShapeDtypeStruct((8, 128), F32),
            jax.ShapeDtypeStruct((5, CH), F32),
        ),
        in_specs=[smem] + [vmem] * 11,
        out_specs=(vmem,) * 7,
        scratch_shapes=[
            pltpu.VMEM((49, 8, CH), F32),
            pltpu.VMEM((14, 144, CH), F32),
            pltpu.VMEM((7, 14, COLS, CH), F32),
            pltpu.VMEM((7, 14, COLS, CH), F32),
            pltpu.VMEM((2, 2, 3, 8, CH), F32),
            *halo_scratch,
            pltpu.VMEM((2, 3, 24, CH), F32),
            pltpu.VMEM((ROWS, COLS, CH), BF16),
            *halo_scratch,
            pltpu.VMEM((ROWS, COLS, CH), F32),
            pltpu.VMEM((ROWS, COLS, CH), F32),
            pltpu.VMEM((ROWS, COLS, 1), F32),
            pltpu.VMEM((cells, CH), BF16),
            pltpu.VMEM((CH, cells), BF16),
            pltpu.VMEM((CH, cells), BF16),
            pltpu.VMEM((cells, HID), F32),
            pltpu.VMEM((cells, HID), BF16),
            pltpu.VMEM((cells, HID), BF16),
            pltpu.VMEM((8, HID), F32),
            pltpu.VMEM((5, 8, CH), F32),
            pltpu.VMEM((2, 128) + tile, BF16),
            pltpu.VMEM((128,) + tile, BF16),
            pltpu.VMEM((128,) + tile, BF16),
            pltpu.VMEM((3, 32) + tile, BF16),
            pltpu.VMEM((32,) + tile, BF16),
            pltpu.VMEM((3, 8) + tile, BF16),
            pltpu.VMEM((8,) + tile, BF16),
            pltpu.VMEM((7,) + tile, BF16),
            pltpu.VMEM((2, 128) + tile, BF16),
            pltpu.VMEM((16, 8, 128), F32),
            pltpu.VMEM((16, 8, 128), F32),
            pltpu.VMEM((16, 8, 128), F32),
            pltpu.VMEM((3, 4, 8, 128), F32),
            pltpu.VMEM((4, 8, 128), F32),
            pltpu.VMEM((3, 8, 128), F32),
            pltpu.VMEM((8, 8, 128), F32),
            pltpu.VMEM((16, 8, 128), F32),
            pltpu.SemaphoreType.DMA((14,)),
            pltpu.SemaphoreType.DMA((14,)),
            pltpu.SemaphoreType.DMA((14,)),
            pltpu.SemaphoreType.DMA((14,)),
            pltpu.SemaphoreType.DMA((28,)),
            pltpu.SemaphoreType.DMA((28,)),
            pltpu.SemaphoreType.DMA((20,)),
            pltpu.SemaphoreType.DMA((20,)),
        ],
        compiler_params=pltpu.CompilerParams(
            collective_id=0, has_side_effects=True, vmem_limit_bytes=62 * 1024 * 1024
        ),
    )(
        edge_match.reshape(-1),
        fields[0],
        cotangent[0],
        depth_kernel,
        depth_bias.reshape(1, CH),
        norm_gain.reshape(1, CH),
        norm_bias.reshape(1, CH),
        expand_weight,
        expand_bias.reshape(1, HID),
        reduce_weight,
        reduce_bias.reshape(1, CH),
        layer_scale.reshape(1, CH),
    )
    return (result[None], gfields[None], gkernel, gexpand, greduce, gbias.reshape(HID), gvectors)


def solution(mesh):
    return jax.shard_map(
        shards,
        mesh=mesh,
        in_specs=(P("face", "tile", None, None),) * 2 + (P(),) * 10,
        out_specs=(P("face", "tile", None, None),) * 2 + (P(),) * 5,
        check_vma=False,
    )
```

```python
import functools
import math

import jax
import jax.numpy as jnp
from jax import lax
from jax.experimental import pallas as pl
from jax.experimental.pallas import tpu as pltpu
from jax.sharding import PartitionSpec as P

EPSILON = 1e-06
ROOT_COEF = 0.7978845608028654
CUBIC_COEF = 0.044715
MESH = pl.DeviceIdType.MESH
FACES = 8
TILES = 32
ROWS = 8
COLS = 128
CH = 256
HID = 1024
F32 = jnp.float32
BF16 = jnp.bfloat16
OWN_PAIRS = [(i, a) for i in range(ROWS) for a in range(7) if 3 <= i + a <= 10]
RIM_PAIRS = [(i, a) for i in range(ROWS) for a in range(7) if not 3 <= i + a <= 10]


def halo_plan(face, tile):
    beside = face + 1 - 2 * lax.rem(face, 2)
    across = lax.rem(face + 4, FACES)
    plan = [
        ("up", (face, lax.rem(tile + TILES - 1, TILES))),
        ("down", (face, lax.rem(tile + 1, TILES))),
    ]
    for link, partner in enumerate((beside, across)):
        for flip in range(2):
            for place in range(3):
                if flip == 0:
                    target = tile + TILES + 1 - place
                else:
                    target = 2 * TILES - tile - place
                plan.append(((link, flip, place), (partner, lax.rem(target, TILES))))
    return plan


def device_at(x, y, z, core):
    return (2 * y + lax.rem(x, 2), 16 * lax.div(x, 2) + 2 * z + core)


class Schedule:
    def __init__(self):
        self.now = 0.0
        self.flows = []

    def add(self, steps, delays):
        self.flows.append([self.now, list(steps), list(delays)])
        self.tick(0.0)

    def step(self, flow):
        flow[1].pop(0)()
        self.now += 0.3
        if flow[1]:
            flow[0] = self.now + flow[2].pop(0)
        else:
            self.flows.remove(flow)

    def tick(self, cost):
        self.now += 1.25 * cost
        while self.flows:
            flow = min(self.flows, key=lambda item: item[0])
            if flow[0] > self.now:
                break
            self.step(flow)

    def drain(self):
        while self.flows:
            flow = min(self.flows, key=lambda item: item[0])
            self.now = max(self.now, flow[0])
            self.step(flow)


def pick(flag, if_one, if_zero):
    return jnp.where(jnp.broadcast_to(flag, if_one.shape) == 1, if_one, if_zero)


def dot_nn(left, right):
    return lax.dot_general(left, right, (((1,), (0,)), ((), ())), preferred_element_type=F32)


def dot_nt(left, right):
    return lax.dot_general(left, right, (((1,), (1,)), ((), ())), preferred_element_type=F32)


def fold(block):
    return jnp.sum(block.reshape(16, 8, block.shape[1]), axis=0)


def conv_chunk(shifted, taps, flipped, out, chunk, pairs, start):
    cols = pl.ds(pl.multiple_of(chunk * 8, 8), 8)
    for half in range(2):
        lanes = slice(half * 128, half * 128 + 128)
        acc = {}
        for i in sorted({i for i, _ in pairs}):
            acc[i] = out[i, cols, lanes] if start is None else start[:, lanes]
        for b in range(7):
            rows = {r: shifted[b, r, cols, lanes] for r in sorted({i + a for i, a in pairs})}
            for a in sorted({a for _, a in pairs}):
                tap = taps[48 - a * 7 - b if flipped else a * 7 + b, :, lanes]
                for i in sorted({i for i, a2 in pairs if a2 == a}):
                    acc[i] = acc[i] + tap * rows[i + a]
        for i, value in acc.items():
            out[i, cols, lanes] = value


def block_kernel(
    edge_ref,
    fields_ref,
    cot_ref,
    taps_ref,
    depth_bias_ref,
    gain_ref,
    norm_bias_ref,
    w1_ref,
    b1_ref,
    w2_ref,
    b2_ref,
    scale_ref,
    result_ref,
    gfields_ref,
    gkernel_ref,
    gexpand_ref,
    greduce_ref,
    gbias_ref,
    gvectors_ref,
    taps,
    wide,
    shifted,
    shifted_g,
    strip_f,
    strips,
    above,
    below,
    ghosts,
    ghost_f,
    rows_g,
    strips_g,
    above_g,
    below_g,
    ghosts_g,
    conv,
    standard,
    inverse,
    normed,
    normed_t,
    cot_branch_t,
    grad_hidden,
    active,
    grad_pre,
    bias_sum,
    vector_sum,
    src,
    from_core,
    sum_core,
    from_plane,
    sum_z,
    gathered,
    small_in,
    small_plane,
    small_line,
    small_out,
    late_in,
    late_line,
    late_plane,
    halo_send,
    halo_recv,
    grad_send,
    grad_recv,
    big_send,
    big_recv,
    small_send,
    small_recv,
    factor,
):
    face, tile = lax.axis_index("face"), lax.axis_index("tile")
    core = lax.rem(tile, 2)
    z = lax.rem(lax.div(tile, 2), 8)
    x = 2 * lax.div(tile, 16) + lax.rem(face, 2)
    y = lax.div(face, 2)
    sibling = device_at(x, y, z, 1 - core)

    mine = 4 * x + y
    lane = 2 * z + core

    def plane_place(step):
        return lax.rem(x + step // 4, 4), lax.rem(y + step % 4, 4)

    def plane_peer(step):
        new_x, new_y = plane_place(step)
        return device_at(new_x, new_y, z, core)

    def z_peer(step):
        return device_at(x, y, lax.rem(z + step, 8), core)

    def line_peer(step):
        new = lax.rem(lane + step, 16)
        return device_at(x, y, lax.div(new, 2), lax.rem(new, 2))

    plan = halo_plan(face, tile)
    barrier = pltpu.get_barrier_semaphore()
    peers = [target for _, target in plan]
    peers += [plane_peer(step) for step in range(1, 16)]
    peers += [line_peer(step) for step in range(1, 16)]
    for peer in peers:
        pl.semaphore_signal(barrier, inc=1, device_id=peer, device_id_type=MESH)

    first = jnp.where(tile == 0, 1, 0)
    last = jnp.where(tile == TILES - 1, 1, 0)
    beside = face + 1 - 2 * lax.rem(face, 2)
    beside_side = jnp.where(edge_ref[0, 0, face] == beside, 0, 1)

    def make_strips(target):
        for row in range(ROWS):
            for depth in range(3):
                for side, col in ((0, 8 + depth), (1, 135 - depth)):
                    piece = wide[3 + row, col : col + 1, :]
                    strip_f[side, 0, depth, row : row + 1, :] = piece
                    strip_f[side, 1, depth, 7 - row : 8 - row, :] = piece
        for flip in range(2):
            for depth in range(3):
                west, east = strip_f[0, flip, depth], strip_f[1, flip, depth]
                target[0, flip, depth] = pick(beside_side, east, west).astype(BF16)
                target[1, flip, depth] = pick(beside_side, west, east).astype(BF16)

    def start_halo(rows, strip, to_above, to_below, to_ghosts, send, recv):
        copies = []
        for index, (kind, target) in enumerate(plan):
            if kind == "up":
                source, landing = rows.at[0:3], to_below
            elif kind == "down":
                source, landing = rows.at[ROWS - 3 : ROWS], to_above
            else:
                link, flip, place = kind
                source, landing = strip.at[link, flip], to_ghosts.at[link, flip, place]
            copy = pltpu.make_async_remote_copy(
                source, landing, send.at[index], recv.at[index], target, MESH
            )
            copy.start()
            copies.append(copy)
        return copies

    def take_ghosts(source):
        for side in range(2):
            reverse = edge_ref[2, side, face]
            other = beside_side if side == 0 else 1 - beside_side
            for place in range(3):
                for depth in range(3):
                    values = [
                        pick(
                            other,
                            source[1, flip, place, depth].astype(F32),
                            source[0, flip, place, depth].astype(F32),
                        )
                        for flip in range(2)
                    ]
                    value = pick(reverse, values[1], values[0])
                    if place == 0:
                        value = pick(first, jnp.zeros_like(value), value)
                    if place == 2:
                        value = pick(last, jnp.zeros_like(value), value)
                    ghost_f[side, depth, place * 8 : place * 8 + 8, :] = value

    def take_rows(source_above, source_below):
        for row in range(3):
            value = source_above[row].astype(F32)
            wide[row, 8:136, :] = pick(first, jnp.zeros_like(value), value)
            value = source_below[row].astype(F32)
            wide[11 + row, 8:136, :] = pick(last, jnp.zeros_like(value), value)

    def shift_row(target, row):
        for b in range(7):
            target[b, row] = wide[row, 5 + b : 133 + b, :]

    for a in range(7):
        block = taps_ref[a].astype(F32)
        for b in range(7):
            taps[a * 7 + b] = jnp.broadcast_to(block[b : b + 1, :], (8, CH))
    edge_zero = jnp.zeros((8, CH), F32)

    def load_row(row, carry):
        wide[3 + row, 0:8, :] = edge_zero
        wide[3 + row, 136:144, :] = edge_zero
        wide[3 + row, 8:136, :] = fields_ref[row].astype(F32)
        return carry

    lax.fori_loop(0, ROWS, load_row, 0)
    make_strips(strips)
    vector_sum[...] = jnp.zeros_like(vector_sum)

    def own_shift(row, carry):
        shift_row(shifted, 3 + row)
        return carry

    lax.fori_loop(0, ROWS, own_shift, 0)
    def cot_row(row, carry):
        cells = pl.ds(pl.multiple_of(row * COLS, COLS), COLS)
        upstream = cot_ref[row].astype(F32)
        scaled = upstream * scale_ref[...]
        half_grad = (0.5 * scaled).astype(BF16)
        cot_branch_t[:, cells] = jnp.transpose(scaled).astype(BF16)
        vector_sum[3] = vector_sum[3] + fold(upstream)
        for part in range(4):
            hidden = slice(part * 256, part * 256 + 256)
            grad_hidden[cells, hidden] = dot_nt(half_grad, w2_ref[hidden, :])
        return carry

    lax.fori_loop(0, ROWS, cot_row, 0)
    pl.semaphore_wait(barrier, len(peers))
    halo = start_halo(fields_ref, strips, above, below, ghosts, halo_send, halo_recv)

    start = jnp.broadcast_to(depth_bias_ref[...], (8, CH))

    def own_conv(chunk, carry):
        conv_chunk(shifted, taps, False, conv, chunk, OWN_PAIRS, start)
        return carry

    lax.fori_loop(1, 15, own_conv, 0)

    halo[0].wait()
    halo[1].wait()
    take_rows(above, below)

    def rim_shift(row, carry):
        shift_row(shifted, row)
        shift_row(shifted, 11 + row)
        return carry

    lax.fori_loop(0, 3, rim_shift, 0)

    def rim_conv(chunk, carry):
        conv_chunk(shifted, taps, False, conv, chunk, RIM_PAIRS, None)
        return carry

    lax.fori_loop(1, 15, rim_conv, 0)
    for copy in halo[2:]:
        copy.wait()
    take_ghosts(ghosts)
    for row in range(14):
        for depth in range(3):
            wide[row, 7 - depth : 8 - depth, :] = ghost_f[0, depth, row + 5 : row + 6, :]
            wide[row, 136 + depth : 137 + depth, :] = ghost_f[1, depth, row + 5 : row + 6, :]

    def edge_shift(row, carry):
        for b in range(7):
            shifted[b, row, 0:8, :] = wide[row, 5 + b : 13 + b, :]
            shifted[b, row, 120:128, :] = wide[row, 125 + b : 133 + b, :]
        return carry

    lax.fori_loop(0, 14, edge_shift, 0)

    def edge_conv(index, carry):
        conv_chunk(shifted, taps, False, conv, index * 15, OWN_PAIRS + RIM_PAIRS, start)
        return carry

    lax.fori_loop(0, 2, edge_conv, 0)

    normed_t[256:272, :] = jnp.ones((16, ROWS * COLS), BF16)

    def norm_row(row, carry):
        cells = pl.ds(pl.multiple_of(row * COLS, COLS), COLS)
        value = conv[row]
        centred = value - jnp.sum(value, axis=1, keepdims=True) * (1.0 / CH)
        variance = jnp.sum(centred * centred, axis=1, keepdims=True) * (1.0 / CH)
        inv = lax.rsqrt(variance + EPSILON)
        std = centred * inv
        standard[row] = std
        inverse[row] = inv
        scaled = std * gain_ref[...] + norm_bias_ref[...]
        normed[cells, :] = (0.5 * scaled).astype(BF16)
        normed_t[0:256, cells] = jnp.transpose(scaled).astype(BF16)
        return carry

    lax.fori_loop(0, ROWS, norm_row, 0)

    schedule = Schedule()

    def part_flow(part):
        counter = [part * 5]
        def send(source, landing, target):
            pltpu.make_async_remote_copy(
                source,
                landing,
                big_send.at[counter[0]],
                big_recv.at[counter[0]],
                target,
                MESH,
            ).start()

        def arrived(like):
            every = pltpu.make_async_remote_copy(
                like, like, big_send.at[counter[0]], big_recv.at[counter[0]], sibling, MESH
            )
            every.wait_send()
            every.wait_recv()
            counter[0] += 1

        def to_core():
            send(src.at[part, 1 - core], from_core.at[part], sibling)

        def to_plane():
            arrived(from_core.at[part])

            def add(index, carry):
                sum_core[part, index] = (
                    src[part, core, index].astype(F32) + from_core[part, index].astype(F32)
                ).astype(BF16)
                return carry

            lax.fori_loop(0, 32, add, 0, unroll=8)
            for step in range(1, 16):
                new_x, new_y = plane_place(step)
                block = sum_core.at[part, pl.ds(8 * new_x + 2 * new_y, 2)]
                send(block, from_plane.at[part, step - 1], plane_peer(step))

        def to_z():
            arrived(from_plane.at[part])
            for index in range(2):
                total = sum_core[part, 2 * mine + index].astype(F32)
                for step in range(15):
                    total = total + from_plane[part, step, index].astype(F32)
                sum_z[part, z, index] = total.astype(BF16)
            for step in range(1, 8):
                send(sum_z.at[part, z], sum_z.at[part, z], z_peer(step))

        def back_plane():
            arrived(sum_z.at[part, 0:7])
            for index in range(2):
                total = sum_z[part, 0, index].astype(F32)
                for step in range(1, 8):
                    total = total + sum_z[part, step, index].astype(F32)
                gathered[part, core, 2 * mine + index] = total.astype(BF16)
            block = gathered.at[part, core, pl.ds(2 * mine, 2)]
            for step in range(1, 16):
                send(block, block, plane_peer(step))

        def back_core():
            arrived(from_plane.at[part])
            send(gathered.at[part, core], gathered.at[part, core], sibling)

        def unpack():
            arrived(gathered.at[part, core])

            def one(row, carry):
                rows = pl.ds(pl.multiple_of(row * 16, 16), 16)
                down = pl.ds(pl.multiple_of(part * 256 + row * 16, 16), 16)
                for col in range(2):
                    across = slice(part * 256 + col * 128, part * 256 + col * 128 + 128)
                    lanes = slice(col * 128, col * 128 + 128)
                    gexpand_ref[rows, across] = gathered[part, 0, row * 2 + col].astype(F32) * factor
                    greduce_ref[down, lanes] = gathered[part, 1, row * 2 + col].astype(F32) * factor
                return carry

            lax.fori_loop(0, 16, one, 0, unroll=4)

        schedule.add(
            [to_core, to_plane, to_z, back_plane, back_core, unpack],
            [1.7, 5.6, 5.6, 5.6, 1.7],
        )

    for part in range(4):
        hidden = slice(part * 256, part * 256 + 256)

        def hidden_row(row, carry):
            cells = pl.ds(pl.multiple_of(row * 256, 256), 256)
            half = dot_nn(normed[cells, :], w1_ref[:, hidden]) + 0.5 * b1_ref[:, hidden]
            square = half * half
            tanhed = jnp.tanh(
                half * (2.0 * ROOT_COEF + (8.0 * ROOT_COEF * CUBIC_COEF) * square)
            )
            plus = 1.0 + tanhed
            value = half * plus
            active[cells, hidden] = value.astype(BF16)
            twice_slope = plus + (value * (1.0 - tanhed)) * (
                2.0 * ROOT_COEF + (24.0 * ROOT_COEF * CUBIC_COEF) * square
            )
            grad_pre[cells, hidden] = (grad_hidden[cells, hidden] * twice_slope).astype(BF16)
            return carry

        lax.fori_loop(0, 2, hidden_row, 0)
        schedule.tick(0.7)
        lax.fori_loop(2, 4, hidden_row, 0)
        schedule.tick(0.7)
        block = dot_nn(normed_t[...], grad_pre[:, hidden])
        bias_sum[:, hidden] = block[256:264, :]
        block = block[0:256, :].astype(BF16)
        for row in range(16):
            for col in range(2):
                src[part, 0, row * 2 + col] = block[
                    row * 16 : row * 16 + 16, col * 128 : col * 128 + 128
                ]
        schedule.tick(0.3)
        block = jnp.transpose(dot_nn(cot_branch_t[...], active[:, hidden])).astype(BF16)
        for row in range(16):
            for col in range(2):
                src[part, 1, row * 2 + col] = block[
                    row * 16 : row * 16 + 16, col * 128 : col * 128 + 128
                ]
        schedule.tick(0.3)
        part_flow(part)

    def grad_row(pair, carry):
        both = dot_nt(grad_pre[pl.ds(pl.multiple_of(pair * 256, 256), 256), :], w1_ref[...])
        for side in range(2):
            row = pair * 2 + side
            grad_normed = both[side * 128 : side * 128 + 128]
            std = standard[row]
            scaled = grad_normed * gain_ref[...]
            mean = jnp.sum(scaled, axis=1, keepdims=True) * (1.0 / CH)
            slant = jnp.sum(scaled * std, axis=1, keepdims=True) * (1.0 / CH)
            grad = (scaled - mean - std * slant) * inverse[row]
            conv[row] = grad
            wide[3 + row, 0:8, :] = edge_zero
            wide[3 + row, 136:144, :] = edge_zero
            wide[3 + row, 8:136, :] = grad
            rows_g[row] = grad.astype(BF16)
            vector_sum[0] = vector_sum[0] + fold(grad)
            vector_sum[1] = vector_sum[1] + fold(grad_normed * std)
            vector_sum[2] = vector_sum[2] + fold(grad_normed)
        return carry

    lax.fori_loop(0, 2, grad_row, 0)
    schedule.tick(0.9)
    lax.fori_loop(2, 4, grad_row, 0)
    make_strips(strips_g)
    halo = start_halo(rows_g, strips_g, above_g, below_g, ghosts_g, grad_send, grad_recv)
    schedule.tick(1.0)

    small_in[...] = jnp.zeros_like(small_in)
    for b in range(7):

        def tap_sums(chunk, carry):
            cols = pl.ds(pl.multiple_of(chunk * 8, 8), 8)
            sums = list(carry)
            for half in range(2):
                lanes = slice(half * 128, half * 128 + 128)
                grads = [conv[i, cols, lanes] for i in range(ROWS)]
                for r in range(14):
                    value = shifted[b, r, cols, lanes]
                    for a in range(7):
                        if 0 <= r - a < ROWS:
                            sums[a * 2 + half] = sums[a * 2 + half] + grads[r - a] * value
            return tuple(sums)

        sums = lax.fori_loop(0, 16, tap_sums, tuple(jnp.zeros((8, 128), F32) for _ in range(14)))
        for index, value in enumerate(sums):
            small_in[index, b : b + 1, :] = jnp.sum(value, axis=0, keepdims=True)
        schedule.tick(0.85)
    for part in range(8):
        small_in[part, 7:8, :] = bias_sum[0:1, part * 128 : part * 128 + 128]
    for row in range(4):
        total = jnp.sum(vector_sum[row], axis=0, keepdims=True)
        if row == 3:
            total = total * scale_ref[...]
        for half in range(2):
            small_in[14 + half, row : row + 1, :] = total[:, half * 128 : half * 128 + 128]

    def small_flow():
        counter = [0]

        def send(source, landing, target):
            pltpu.make_async_remote_copy(
                source,
                landing,
                small_send.at[counter[0]],
                small_recv.at[counter[0]],
                target,
                MESH,
            ).start()

        def arrived(like):
            every = pltpu.make_async_remote_copy(
                like, like, small_send.at[counter[0]], small_recv.at[counter[0]], sibling, MESH
            )
            every.wait_send()
            every.wait_recv()
            counter[0] += 1

        def to_plane():
            for step in range(1, 16):
                new_x, new_y = plane_place(step)
                send(small_in.at[4 * new_x + new_y], small_plane.at[step - 1], plane_peer(step))

        def to_line():
            arrived(small_plane)
            total = small_in[mine]
            for step in range(15):
                total = total + small_plane[step]
            small_line[lane] = total
            for step in range(1, 16):
                send(small_line.at[lane], small_line.at[lane], line_peer(step))

        def back_plane():
            arrived(small_plane)
            total = small_line[0]
            for step in range(1, 16):
                total = total + small_line[step]
            small_out[mine] = total * factor
            for step in range(1, 16):
                send(small_out.at[mine], small_out.at[mine], plane_peer(step))

        def unpack():
            arrived(small_plane)
            for a in range(7):
                for half in range(2):
                    lanes = slice(half * 128, half * 128 + 128)
                    gkernel_ref[a, :, lanes] = small_out[2 * a + half, 0:7, :]
            for part in range(8):
                gbias_ref[part : part + 1, :] = small_out[part, 7:8, :]
            for half in range(2):
                lanes = slice(half * 128, half * 128 + 128)
                gvectors_ref[0:4, lanes] = small_out[14 + half, 0:4, :]

        schedule.add(
            [to_plane, to_line, back_plane, unpack], [5.0, 5.5, 5.0]
        )

    small_flow()

    def result_row(pair, carry):
        both = dot_nn(active[pl.ds(pl.multiple_of(pair * 256, 256), 256), :], w2_ref[...])
        for side in range(2):
            row = pair * 2 + side
            branch = both[side * 128 : side * 128 + 128] + b2_ref[...]
            result_ref[row] = (fields_ref[row].astype(F32) + scale_ref[...] * branch).astype(BF16)
            vector_sum[4] = vector_sum[4] + fold(cot_ref[row].astype(F32) * branch)
        return carry

    lax.fori_loop(0, 2, result_row, 0)
    schedule.tick(0.6)
    lax.fori_loop(2, 4, result_row, 0)
    schedule.tick(0.6)

    late_in[...] = jnp.zeros_like(late_in)
    total = jnp.sum(vector_sum[4], axis=0, keepdims=True)
    for half in range(2):
        late_in[half, 0:1, :] = total[:, half * 128 : half * 128 + 128]

    def late_flow():
        counter = [3]

        def send(source, landing, target):
            pltpu.make_async_remote_copy(
                source,
                landing,
                small_send.at[counter[0]],
                small_recv.at[counter[0]],
                target,
                MESH,
            ).start()

        def arrived(like):
            every = pltpu.make_async_remote_copy(
                like, like, small_send.at[counter[0]], small_recv.at[counter[0]], sibling, MESH
            )
            every.wait_send()
            every.wait_recv()
            counter[0] += 1

        def to_line():
            late_line[lane] = late_in[...]
            for step in range(1, 16):
                send(late_line.at[lane], late_line.at[lane], line_peer(step))

        def to_plane():
            arrived(late_line.at[0:15])
            total = late_line[0]
            for step in range(1, 16):
                total = total + late_line[step]
            late_plane[mine] = total
            for step in range(1, 16):
                send(late_plane.at[mine], late_plane.at[mine], plane_peer(step))

        def unpack():
            arrived(late_plane.at[0:15])
            total = late_plane[0]
            for step in range(1, 16):
                total = total + late_plane[step]
            for half in range(2):
                lanes = slice(half * 128, half * 128 + 128)
                gvectors_ref[4:5, lanes] = total[half, 0:1, :] * factor

        schedule.add([to_line, to_plane, unpack], [5.5, 5.0])

    late_flow()

    def own_shift_g(row, carry):
        shift_row(shifted_g, 3 + row)
        return carry

    def own_conv_g(chunk, carry):
        conv_chunk(shifted_g, taps, True, conv, chunk, OWN_PAIRS, edge_zero)
        return carry

    lax.fori_loop(0, ROWS, own_shift_g, 0)
    schedule.tick(0.65)
    for quarter in range(4):
        lax.fori_loop(quarter * 4, quarter * 4 + 4, own_conv_g, 0)
        schedule.tick(1.1)
    halo[0].wait()
    halo[1].wait()
    take_rows(above_g, below_g)
    for row in range(3):
        for side_row in (row, 11 + row):
            wide[side_row, 0:8, :] = edge_zero
            wide[side_row, 136:144, :] = edge_zero

    def rim_shift_g(row, carry):
        shift_row(shifted_g, row)
        shift_row(shifted_g, 11 + row)
        return carry

    def rim_conv_g(chunk, carry):
        conv_chunk(shifted_g, taps, True, conv, chunk, RIM_PAIRS, None)
        return carry

    lax.fori_loop(0, 3, rim_shift_g, 0)
    schedule.tick(0.6)
    lax.fori_loop(0, 8, rim_conv_g, 0)
    schedule.tick(0.8)
    lax.fori_loop(8, 16, rim_conv_g, 0)
    schedule.tick(0.8)
    for copy in halo[2:]:
        copy.wait()
    take_ghosts(ghosts_g)
    for side in range(2):
        partner_side = edge_ref[1, side, face]
        reverse = edge_ref[2, side, face]
        totals = [jnp.zeros((8, CH), F32) for _ in range(3)]
        for a in range(7):
            weights = []
            for offset in range(1, 4):
                weights.append(
                    pick(
                        partner_side,
                        pick(reverse, taps[(6 - a) * 7 + 3 + offset], taps[a * 7 + 3 + offset]),
                        pick(reverse, taps[(6 - a) * 7 + 3 - offset], taps[a * 7 + 3 - offset]),
                    )
                )
            for other in range(3):
                value = ghost_f[side, other, 11 - a : 19 - a, :]
                for depth in range(3 - other):
                    totals[depth] = totals[depth] + weights[depth + other] * value
        for depth in range(3):
            strip_f[side, 0, depth] = totals[depth]
            col = depth if side == 0 else COLS - 1 - depth
            for row in range(ROWS):
                conv[row, col : col + 1, :] = (
                    conv[row, col : col + 1, :] + strip_f[side, 0, depth, row : row + 1, :]
                )
    schedule.tick(0.5)

    def fields_row(row, carry):
        gfields_ref[row] = (conv[row] + cot_ref[row].astype(F32)).astype(BF16)
        return carry

    lax.fori_loop(0, ROWS, fields_row, 0)
    schedule.tick(0.2)
    schedule.drain()


def copy_out(*refs):
    count = len(refs) // 2
    sems = refs[-1]
    copies = [
        pltpu.make_async_copy(refs[index], refs[count + index], sems.at[index])
        for index in range(count)
    ]
    for copy in copies:
        copy.start()
    for copy in copies:
        copy.wait()


def shards(
    fields,
    cotangent,
    edge_match,
    depth_kernel,
    depth_bias,
    norm_gain,
    norm_bias,
    expand_weight,
    expand_bias,
    reduce_weight,
    reduce_bias,
    layer_scale,
):
    vmem = pl.BlockSpec(memory_space=pltpu.VMEM)
    smem = pl.BlockSpec(memory_space=pltpu.SMEM)
    tile = (16, 128)
    cells = ROWS * COLS
    factor = 1.0 / math.sqrt(FACES * TILES * cells)
    halo_scratch = [
        pltpu.VMEM((2, 2, 3, 8, CH), BF16),
        pltpu.VMEM((3, COLS, CH), BF16),
        pltpu.VMEM((3, COLS, CH), BF16),
        pltpu.VMEM((2, 2, 3, 3, 8, CH), BF16),
    ]
    outputs = pl.pallas_call(
        functools.partial(block_kernel, factor=factor),
        out_shape=(
            jax.ShapeDtypeStruct((ROWS, COLS, CH), BF16),
            jax.ShapeDtypeStruct((ROWS, COLS, CH), BF16),
            jax.ShapeDtypeStruct((7, 7, CH), F32),
            jax.ShapeDtypeStruct((CH, HID), F32),
            jax.ShapeDtypeStruct((HID, CH), F32),
            jax.ShapeDtypeStruct((8, 128), F32),
            jax.ShapeDtypeStruct((5, CH), F32),
        ),
        in_specs=[smem] + [vmem] * 11,
        out_specs=(vmem,) * 7,
        scratch_shapes=[
            pltpu.VMEM((49, 8, CH), F32),
            pltpu.VMEM((14, 144, CH), F32),
            pltpu.VMEM((7, 14, COLS, CH), F32),
            pltpu.VMEM((7, 14, COLS, CH), F32),
            pltpu.VMEM((2, 2, 3, 8, CH), F32),
            *halo_scratch,
            pltpu.VMEM((2, 3, 24, CH), F32),
            pltpu.VMEM((ROWS, COLS, CH), BF16),
            *halo_scratch,
            pltpu.VMEM((ROWS, COLS, CH), F32),
            pltpu.VMEM((ROWS, COLS, CH), F32),
            pltpu.VMEM((ROWS, COLS, 1), F32),
            pltpu.VMEM((cells, CH), BF16),
            pltpu.VMEM((CH + 16, cells), BF16),
            pltpu.VMEM((CH, cells), BF16),
            pltpu.VMEM((cells, HID), F32),
            pltpu.VMEM((cells, HID), BF16),
            pltpu.VMEM((cells, HID), BF16),
            pltpu.VMEM((8, HID), F32),
            pltpu.VMEM((5, 8, CH), F32),
            pltpu.VMEM((4, 2, 32) + tile, BF16),
            pltpu.VMEM((4, 32) + tile, BF16),
            pltpu.VMEM((4, 32) + tile, BF16),
            pltpu.VMEM((4, 15, 2) + tile, BF16),
            pltpu.VMEM((4, 8, 2) + tile, BF16),
            pltpu.VMEM((4, 2, 32) + tile, BF16),
            pltpu.VMEM((16, 8, 128), F32),
            pltpu.VMEM((15, 8, 128), F32),
            pltpu.VMEM((16, 8, 128), F32),
            pltpu.VMEM((16, 8, 128), F32),
            pltpu.VMEM((2, 8, 128), F32),
            pltpu.VMEM((16, 2, 8, 128), F32),
            pltpu.VMEM((16, 2, 8, 128), F32),
            pltpu.SemaphoreType.DMA((14,)),
            pltpu.SemaphoreType.DMA((14,)),
            pltpu.SemaphoreType.DMA((14,)),
            pltpu.SemaphoreType.DMA((14,)),
            pltpu.SemaphoreType.DMA((20,)),
            pltpu.SemaphoreType.DMA((20,)),
            pltpu.SemaphoreType.DMA((5,)),
            pltpu.SemaphoreType.DMA((5,)),
        ],
        compiler_params=pltpu.CompilerParams(
            collective_id=0, has_side_effects=True, vmem_limit_bytes=54 * 1024 * 1024
        ),
    )(
        edge_match.transpose(2, 1, 0),
        fields[0],
        cotangent[0],
        depth_kernel,
        depth_bias.reshape(1, CH),
        norm_gain.reshape(1, CH),
        norm_bias.reshape(1, CH),
        expand_weight,
        expand_bias.reshape(1, HID),
        reduce_weight,
        reduce_bias.reshape(1, CH),
        layer_scale.reshape(1, CH),
    )
    anywhere = pl.BlockSpec(memory_space=pl.ANY)
    result, gfields, gkernel, gexpand, greduce, gbias, gvectors = pl.pallas_call(
        copy_out,
        out_shape=tuple(jax.ShapeDtypeStruct(item.shape, item.dtype) for item in outputs),
        in_specs=[vmem] * 7,
        out_specs=(anywhere,) * 7,
        scratch_shapes=[pltpu.SemaphoreType.DMA((7,))],
    )(*outputs)
    return (result[None], gfields[None], gkernel, gexpand, greduce, gbias.reshape(HID), gvectors)


def solution(mesh):
    return jax.shard_map(
        shards,
        mesh=mesh,
        in_specs=(P("face", "tile", None, None),) * 2 + (P(),) * 10,
        out_specs=(P("face", "tile", None, None),) * 2 + (P(),) * 5,
        check_vma=False,
    )
```

```python
import functools
import math

import jax
import jax.numpy as jnp
from jax import lax
from jax.experimental import pallas as pl
from jax.experimental.pallas import tpu as pltpu
from jax.sharding import PartitionSpec as P

EPSILON = 1e-06
ROOT_COEF = 0.7978845608028654
CUBIC_COEF = 0.044715
MESH = pl.DeviceIdType.MESH
FACES = 8
TILES = 32
ROWS = 8
COLS = 128
CH = 256
HID = 1024
F32 = jnp.float32
BF16 = jnp.bfloat16
OWN_PAIRS = [(i, a) for i in range(ROWS) for a in range(7) if 3 <= i + a <= 10]
RIM_PAIRS = [(i, a) for i in range(ROWS) for a in range(7) if not 3 <= i + a <= 10]


def halo_plan(face, tile):
    beside = face + 1 - 2 * lax.rem(face, 2)
    across = lax.rem(face + 4, FACES)
    plan = [
        ("up", (face, lax.rem(tile + TILES - 1, TILES))),
        ("down", (face, lax.rem(tile + 1, TILES))),
    ]
    for link, partner in enumerate((beside, across)):
        for flip in range(2):
            for place in range(3):
                if flip == 0:
                    target = tile + TILES + 1 - place
                else:
                    target = 2 * TILES - tile - place
                plan.append(((link, flip, place), (partner, lax.rem(target, TILES))))
    return plan


def device_at(x, y, z, core):
    return (2 * y + lax.rem(x, 2), 16 * lax.div(x, 2) + 2 * z + core)


class Schedule:
    def __init__(self):
        self.now = 0.0
        self.flows = []

    def add(self, steps, delays):
        self.flows.append([self.now, list(steps), list(delays)])
        self.tick(0.0)

    def step(self, flow):
        flow[1].pop(0)()
        self.now += 0.3
        if flow[1]:
            flow[0] = self.now + 2.4 * flow[2].pop(0)
        else:
            self.flows.remove(flow)

    def tick(self, cost):
        self.now += 1.25 * cost
        while self.flows:
            flow = min(self.flows, key=lambda item: item[0])
            if flow[0] > self.now:
                break
            self.step(flow)

    def drain(self):
        while self.flows:
            flow = min(self.flows, key=lambda item: item[0])
            self.now = max(self.now, flow[0])
            self.step(flow)


def pick(flag, if_one, if_zero):
    return jnp.where(jnp.broadcast_to(flag, if_one.shape) == 1, if_one, if_zero)


def dot_nn(left, right):
    return lax.dot_general(left, right, (((1,), (0,)), ((), ())), preferred_element_type=F32)


def dot_nt(left, right):
    return lax.dot_general(left, right, (((1,), (1,)), ((), ())), preferred_element_type=F32)


def fold(block):
    return jnp.sum(block.reshape(16, 8, block.shape[1]), axis=0)


def conv_chunk(shifted, taps, flipped, out, chunk, pairs, start):
    cols = pl.ds(pl.multiple_of(chunk * 8, 8), 8)
    for half in range(2):
        lanes = slice(half * 128, half * 128 + 128)
        acc = {}
        for i in sorted({i for i, _ in pairs}):
            acc[i] = out[i, cols, lanes] if start is None else start[:, lanes]
        for b in range(7):
            rows = {r: shifted[b, r, cols, lanes] for r in sorted({i + a for i, a in pairs})}
            for a in sorted({a for _, a in pairs}):
                tap = taps[48 - a * 7 - b if flipped else a * 7 + b, :, lanes]
                for i in sorted({i for i, a2 in pairs if a2 == a}):
                    acc[i] = acc[i] + tap * rows[i + a]
        for i, value in acc.items():
            out[i, cols, lanes] = value


def block_kernel(
    edge_ref,
    fields_ref,
    cot_ref,
    taps_ref,
    depth_bias_ref,
    gain_ref,
    norm_bias_ref,
    w1_ref,
    b1_ref,
    w2_ref,
    b2_ref,
    scale_ref,
    result_ref,
    gfields_ref,
    gkernel_ref,
    gexpand_ref,
    greduce_ref,
    gbias_ref,
    gvectors_ref,
    taps,
    wide,
    shifted,
    shifted_g,
    strip_f,
    strips,
    above,
    below,
    ghosts,
    ghost_f,
    rows_g,
    strips_g,
    above_g,
    below_g,
    ghosts_g,
    conv,
    standard,
    inverse,
    normed,
    normed_t,
    cot_branch_t,
    grad_hidden,
    active,
    grad_pre,
    bias_sum,
    vector_sum,
    src,
    from_core,
    sum_core,
    from_plane,
    sum_z,
    gathered,
    small_in,
    small_plane,
    small_line,
    small_out,
    halo_send,
    halo_recv,
    grad_send,
    grad_recv,
    big_send,
    big_recv,
    small_send,
    small_recv,
    factor,
):
    face, tile = lax.axis_index("face"), lax.axis_index("tile")
    core = lax.rem(tile, 2)
    z = lax.rem(lax.div(tile, 2), 8)
    x = 2 * lax.div(tile, 16) + lax.rem(face, 2)
    y = lax.div(face, 2)
    sibling = device_at(x, y, z, 1 - core)

    mine = 4 * x + y
    lane = 2 * z + core

    def plane_place(step):
        return lax.rem(x + step // 4, 4), lax.rem(y + step % 4, 4)

    def plane_peer(step):
        new_x, new_y = plane_place(step)
        return device_at(new_x, new_y, z, core)

    def z_peer(step):
        return device_at(x, y, lax.rem(z + step, 8), core)

    def line_peer(step):
        new = lax.rem(lane + step, 16)
        return device_at(x, y, lax.div(new, 2), lax.rem(new, 2))

    plan = halo_plan(face, tile)
    barrier = pltpu.get_barrier_semaphore()
    peers = [target for _, target in plan]
    peers += [plane_peer(step) for step in range(1, 16)]
    peers += [line_peer(step) for step in range(1, 16)]
    for peer in peers:
        pl.semaphore_signal(barrier, inc=1, device_id=peer, device_id_type=MESH)

    first = jnp.where(tile == 0, 1, 0)
    last = jnp.where(tile == TILES - 1, 1, 0)
    beside = face + 1 - 2 * lax.rem(face, 2)
    beside_side = jnp.where(edge_ref[0, 0, face] == beside, 0, 1)

    def make_strips(target):
        for row in range(ROWS):
            for depth in range(3):
                for side, col in ((0, 8 + depth), (1, 135 - depth)):
                    piece = wide[3 + row, col : col + 1, :]
                    strip_f[side, 0, depth, row : row + 1, :] = piece
                    strip_f[side, 1, depth, 7 - row : 8 - row, :] = piece
        for flip in range(2):
            for depth in range(3):
                west, east = strip_f[0, flip, depth], strip_f[1, flip, depth]
                target[0, flip, depth] = pick(beside_side, east, west).astype(BF16)
                target[1, flip, depth] = pick(beside_side, west, east).astype(BF16)

    def start_halo(rows, strip, to_above, to_below, to_ghosts, send, recv):
        copies = []
        for index in sorted(range(14), key=lambda i: (i < 2, i < 14 and i >= 2 and plan[i][0][1] == 0)):
            kind, target = plan[index]
            if kind == "up":
                source, landing = rows.at[0:3], to_below
            elif kind == "down":
                source, landing = rows.at[ROWS - 3 : ROWS], to_above
            else:
                link, flip, place = kind
                source, landing = strip.at[link, flip], to_ghosts.at[link, flip, place]
            copy = pltpu.make_async_remote_copy(
                source, landing, send.at[index], recv.at[index], target, MESH
            )
            copy.start()
            copies.append((index, copy))
        return [copy for _, copy in sorted(copies, key=lambda item: item[0])]

    def take_ghosts(source):
        for side in range(2):
            reverse = edge_ref[2, side, face]
            other = beside_side if side == 0 else 1 - beside_side
            for place in range(3):
                for depth in range(3):
                    values = [
                        pick(
                            other,
                            source[1, flip, place, depth].astype(F32),
                            source[0, flip, place, depth].astype(F32),
                        )
                        for flip in range(2)
                    ]
                    value = pick(reverse, values[1], values[0])
                    if place == 0:
                        value = pick(first, jnp.zeros_like(value), value)
                    if place == 2:
                        value = pick(last, jnp.zeros_like(value), value)
                    ghost_f[side, depth, place * 8 : place * 8 + 8, :] = value

    def take_rows(source_above, source_below):
        for row in range(3):
            value = source_above[row].astype(F32)
            wide[row, 8:136, :] = pick(first, jnp.zeros_like(value), value)
            value = source_below[row].astype(F32)
            wide[11 + row, 8:136, :] = pick(last, jnp.zeros_like(value), value)

    def shift_row(target, row):
        for b in range(7):
            target[b, row] = wide[row, 5 + b : 133 + b, :]

    for a in range(7):
        block = taps_ref[a].astype(F32)
        for b in range(7):
            taps[a * 7 + b] = jnp.broadcast_to(block[b : b + 1, :], (8, CH))
    edge_zero = jnp.zeros((8, CH), F32)

    def load_row(row, carry):
        wide[3 + row, 0:8, :] = edge_zero
        wide[3 + row, 136:144, :] = edge_zero
        wide[3 + row, 8:136, :] = fields_ref[row].astype(F32)
        return carry

    lax.fori_loop(0, ROWS, load_row, 0)
    make_strips(strips)
    vector_sum[...] = jnp.zeros_like(vector_sum)

    def own_shift(row, carry):
        shift_row(shifted, 3 + row)
        return carry

    lax.fori_loop(0, ROWS, own_shift, 0)
    def cot_row(row, carry):
        cells = pl.ds(pl.multiple_of(row * COLS, COLS), COLS)
        upstream = cot_ref[row].astype(F32)
        scaled = upstream * scale_ref[...]
        half_grad = (0.5 * scaled).astype(BF16)
        cot_branch_t[:, cells] = jnp.transpose(scaled).astype(BF16)
        vector_sum[3] = vector_sum[3] + fold(upstream)
        for part in range(4):
            hidden = slice(part * 256, part * 256 + 256)
            grad_hidden[cells, hidden] = dot_nt(half_grad, w2_ref[hidden, :])
        return carry

    lax.fori_loop(0, ROWS, cot_row, 0)
    pl.semaphore_wait(barrier, len(peers))
    halo = start_halo(fields_ref, strips, above, below, ghosts, halo_send, halo_recv)

    start = jnp.broadcast_to(depth_bias_ref[...], (8, CH))

    def own_conv(chunk, carry):
        conv_chunk(shifted, taps, False, conv, chunk, OWN_PAIRS, start)
        return carry

    lax.fori_loop(1, 15, own_conv, 0)

    halo[0].wait()
    halo[1].wait()
    take_rows(above, below)

    def rim_shift(row, carry):
        shift_row(shifted, row)
        shift_row(shifted, 11 + row)
        return carry

    lax.fori_loop(0, 3, rim_shift, 0)

    def rim_conv(chunk, carry):
        conv_chunk(shifted, taps, False, conv, chunk, RIM_PAIRS, None)
        return carry

    lax.fori_loop(1, 15, rim_conv, 0)
    for copy in halo[2:]:
        copy.wait()
    take_ghosts(ghosts)
    for row in range(14):
        for depth in range(3):
            wide[row, 7 - depth : 8 - depth, :] = ghost_f[0, depth, row + 5 : row + 6, :]
            wide[row, 136 + depth : 137 + depth, :] = ghost_f[1, depth, row + 5 : row + 6, :]

    def edge_shift(row, carry):
        for b in range(7):
            shifted[b, row, 0:8, :] = wide[row, 5 + b : 13 + b, :]
            shifted[b, row, 120:128, :] = wide[row, 125 + b : 133 + b, :]
        return carry

    lax.fori_loop(0, 14, edge_shift, 0)

    def edge_conv(index, carry):
        conv_chunk(shifted, taps, False, conv, index * 15, OWN_PAIRS + RIM_PAIRS, start)
        return carry

    lax.fori_loop(0, 2, edge_conv, 0)

    normed_t[256:272, :] = jnp.ones((16, ROWS * COLS), BF16)

    def norm_row(row, carry):
        cells = pl.ds(pl.multiple_of(row * COLS, COLS), COLS)
        value = conv[row]
        centred = value - jnp.sum(value, axis=1, keepdims=True) * (1.0 / CH)
        variance = jnp.sum(centred * centred, axis=1, keepdims=True) * (1.0 / CH)
        inv = lax.rsqrt(variance + EPSILON)
        std = centred * inv
        standard[row] = std
        inverse[row] = inv
        scaled = std * gain_ref[...] + norm_bias_ref[...]
        normed[cells, :] = (0.5 * scaled).astype(BF16)
        normed_t[0:256, cells] = jnp.transpose(scaled).astype(BF16)
        return carry

    lax.fori_loop(0, ROWS, norm_row, 0)

    schedule = Schedule()

    def part_flow(part):
        counter = [part * 5]
        def send(source, landing, target):
            pltpu.make_async_remote_copy(
                source,
                landing,
                big_send.at[counter[0]],
                big_recv.at[counter[0]],
                target,
                MESH,
            ).start()

        def arrived(like):
            every = pltpu.make_async_remote_copy(
                like, like, big_send.at[counter[0]], big_recv.at[counter[0]], sibling, MESH
            )
            every.wait_send()
            every.wait_recv()
            counter[0] += 1

        def to_core():
            send(src.at[part, 1 - core], from_core.at[part], sibling)

        def to_plane():
            arrived(from_core.at[part])

            def add(index, carry):
                sum_core[part, index] = (
                    src[part, core, index].astype(F32) + from_core[part, index].astype(F32)
                ).astype(BF16)
                return carry

            lax.fori_loop(0, 32, add, 0, unroll=8)
            for step in range(1, 16):
                new_x, new_y = plane_place(step)
                block = sum_core.at[part, pl.ds(8 * new_x + 2 * new_y, 2)]
                send(block, from_plane.at[part, step - 1], plane_peer(step))

        def to_z():
            arrived(from_plane.at[part])
            for index in range(2):
                total = sum_core[part, 2 * mine + index].astype(F32)
                for step in range(15):
                    total = total + from_plane[part, step, index].astype(F32)
                sum_z[part, z, index] = total.astype(BF16)
            for step in range(1, 8):
                send(sum_z.at[part, z], sum_z.at[part, z], z_peer(step))

        def back_plane():
            arrived(sum_z.at[part, 0:7])
            for index in range(2):
                total = sum_z[part, 0, index].astype(F32)
                for step in range(1, 8):
                    total = total + sum_z[part, step, index].astype(F32)
                gathered[part, core, 2 * mine + index] = total.astype(BF16)
            block = gathered.at[part, core, pl.ds(2 * mine, 2)]
            for step in range(1, 16):
                send(block, block, plane_peer(step))

        def back_core():
            arrived(from_plane.at[part])
            send(gathered.at[part, core], gathered.at[part, core], sibling)

        def unpack():
            arrived(gathered.at[part, core])

            def one(row, carry):
                rows = pl.ds(pl.multiple_of(row * 16, 16), 16)
                down = pl.ds(pl.multiple_of(part * 256 + row * 16, 16), 16)
                for col in range(2):
                    across = slice(part * 256 + col * 128, part * 256 + col * 128 + 128)
                    lanes = slice(col * 128, col * 128 + 128)
                    gexpand_ref[rows, across] = gathered[part, 0, row * 2 + col].astype(F32) * factor
                    greduce_ref[down, lanes] = gathered[part, 1, row * 2 + col].astype(F32) * factor
                return carry

            lax.fori_loop(0, 16, one, 0, unroll=4)

        schedule.add(
            [to_core, to_plane, to_z, back_plane, back_core, unpack],
            [1.7, 5.6, 5.6, 5.6, 1.7],
        )

    for part in range(4):
        hidden = slice(part * 256, part * 256 + 256)

        def hidden_row(row, carry):
            cells = pl.ds(pl.multiple_of(row * 256, 256), 256)
            half = dot_nn(normed[cells, :], w1_ref[:, hidden]) + 0.5 * b1_ref[:, hidden]
            square = half * half
            tanhed = jnp.tanh(
                half * (2.0 * ROOT_COEF + (8.0 * ROOT_COEF * CUBIC_COEF) * square)
            )
            plus = 1.0 + tanhed
            value = half * plus
            active[cells, hidden] = value.astype(BF16)
            twice_slope = plus + (value * (1.0 - tanhed)) * (
                2.0 * ROOT_COEF + (24.0 * ROOT_COEF * CUBIC_COEF) * square
            )
            grad_pre[cells, hidden] = (grad_hidden[cells, hidden] * twice_slope).astype(BF16)
            return carry

        lax.fori_loop(0, 2, hidden_row, 0)
        schedule.tick(0.7)
        lax.fori_loop(2, 4, hidden_row, 0)
        schedule.tick(0.7)
        block = dot_nn(normed_t[...], grad_pre[:, hidden])
        bias_sum[:, hidden] = block[256:264, :]
        block = block[0:256, :].astype(BF16)
        for row in range(16):
            for col in range(2):
                src[part, 0, row * 2 + col] = block[
                    row * 16 : row * 16 + 16, col * 128 : col * 128 + 128
                ]
        schedule.tick(0.3)
        block = jnp.transpose(dot_nn(cot_branch_t[...], active[:, hidden])).astype(BF16)
        for row in range(16):
            for col in range(2):
                src[part, 1, row * 2 + col] = block[
                    row * 16 : row * 16 + 16, col * 128 : col * 128 + 128
                ]
        schedule.tick(0.3)
        part_flow(part)

    def grad_row(pair, carry):
        both = dot_nt(grad_pre[pl.ds(pl.multiple_of(pair * 256, 256), 256), :], w1_ref[...])
        for side in range(2):
            row = pair * 2 + side
            grad_normed = both[side * 128 : side * 128 + 128]
            std = standard[row]
            scaled = grad_normed * gain_ref[...]
            mean = jnp.sum(scaled, axis=1, keepdims=True) * (1.0 / CH)
            slant = jnp.sum(scaled * std, axis=1, keepdims=True) * (1.0 / CH)
            grad = (scaled - mean - std * slant) * inverse[row]
            conv[row] = grad
            wide[3 + row, 0:8, :] = edge_zero
            wide[3 + row, 136:144, :] = edge_zero
            wide[3 + row, 8:136, :] = grad
            rows_g[row] = grad.astype(BF16)
            vector_sum[0] = vector_sum[0] + fold(grad)
            vector_sum[1] = vector_sum[1] + fold(grad_normed * std)
            vector_sum[2] = vector_sum[2] + fold(grad_normed)
        return carry

    lax.fori_loop(0, 2, grad_row, 0)
    schedule.tick(0.9)
    lax.fori_loop(2, 4, grad_row, 0)
    make_strips(strips_g)
    halo = start_halo(rows_g, strips_g, above_g, below_g, ghosts_g, grad_send, grad_recv)
    schedule.tick(1.0)

    def result_row(pair, carry):
        both = dot_nn(active[pl.ds(pl.multiple_of(pair * 256, 256), 256), :], w2_ref[...])
        for side in range(2):
            row = pair * 2 + side
            branch = both[side * 128 : side * 128 + 128] + b2_ref[...]
            result_ref[row] = (fields_ref[row].astype(F32) + scale_ref[...] * branch).astype(BF16)
            vector_sum[4] = vector_sum[4] + fold(cot_ref[row].astype(F32) * branch)
        return carry

    lax.fori_loop(0, 2, result_row, 0)
    schedule.tick(0.6)
    lax.fori_loop(2, 4, result_row, 0)
    schedule.tick(0.6)

    small_in[...] = jnp.zeros_like(small_in)
    for b in range(7):

        def tap_sums(chunk, carry):
            cols = pl.ds(pl.multiple_of(chunk * 8, 8), 8)
            sums = list(carry)
            for half in range(2):
                lanes = slice(half * 128, half * 128 + 128)
                grads = [conv[i, cols, lanes] for i in range(ROWS)]
                for r in range(14):
                    value = shifted[b, r, cols, lanes]
                    for a in range(7):
                        if 0 <= r - a < ROWS:
                            sums[a * 2 + half] = sums[a * 2 + half] + grads[r - a] * value
            return tuple(sums)

        sums = lax.fori_loop(0, 16, tap_sums, tuple(jnp.zeros((8, 128), F32) for _ in range(14)))
        for index, value in enumerate(sums):
            small_in[index, b : b + 1, :] = jnp.sum(value, axis=0, keepdims=True)
        schedule.tick(0.85)
    for part in range(8):
        small_in[part, 7:8, :] = bias_sum[0:1, part * 128 : part * 128 + 128]
    for row in range(5):
        total = jnp.sum(vector_sum[row], axis=0, keepdims=True)
        if row == 3:
            total = total * scale_ref[...]
        for half in range(2):
            small_in[14 + half, row : row + 1, :] = total[:, half * 128 : half * 128 + 128]

    def small_flow():
        counter = [0]

        def send(source, landing, target):
            pltpu.make_async_remote_copy(
                source,
                landing,
                small_send.at[counter[0]],
                small_recv.at[counter[0]],
                target,
                MESH,
            ).start()

        def arrived(like):
            every = pltpu.make_async_remote_copy(
                like, like, small_send.at[counter[0]], small_recv.at[counter[0]], sibling, MESH
            )
            every.wait_send()
            every.wait_recv()
            counter[0] += 1

        def to_plane():
            for step in range(1, 16):
                new_x, new_y = plane_place(step)
                send(small_in.at[4 * new_x + new_y], small_plane.at[step - 1], plane_peer(step))

        def to_line():
            arrived(small_plane)
            total = small_in[mine]
            for step in range(15):
                total = total + small_plane[step]
            small_line[lane] = total
            for step in range(1, 16):
                send(small_line.at[lane], small_line.at[lane], line_peer(step))

        def back_plane():
            arrived(small_plane)
            total = small_line[0]
            for step in range(1, 16):
                total = total + small_line[step]
            small_out[mine] = total * factor
            for step in range(1, 16):
                send(small_out.at[mine], small_out.at[mine], plane_peer(step))

        def unpack():
            arrived(small_plane)
            for a in range(7):
                for half in range(2):
                    lanes = slice(half * 128, half * 128 + 128)
                    gkernel_ref[a, :, lanes] = small_out[2 * a + half, 0:7, :]
            for part in range(8):
                gbias_ref[part : part + 1, :] = small_out[part, 7:8, :]
            for half in range(2):
                lanes = slice(half * 128, half * 128 + 128)
                gvectors_ref[:, lanes] = small_out[14 + half, 0:5, :]

        schedule.add(
            [to_plane, to_line, back_plane, unpack], [5.0, 5.5, 5.0]
        )

    small_flow()

    def own_shift_g(row, carry):
        shift_row(shifted_g, 3 + row)
        return carry

    def own_conv_g(chunk, carry):
        conv_chunk(shifted_g, taps, True, conv, chunk, OWN_PAIRS, edge_zero)
        return carry

    lax.fori_loop(0, ROWS, own_shift_g, 0)
    schedule.tick(0.65)
    for quarter in range(4):
        lax.fori_loop(quarter * 4, quarter * 4 + 4, own_conv_g, 0)
        schedule.tick(1.1)
    halo[0].wait()
    halo[1].wait()
    take_rows(above_g, below_g)
    for row in range(3):
        for side_row in (row, 11 + row):
            wide[side_row, 0:8, :] = edge_zero
            wide[side_row, 136:144, :] = edge_zero

    def rim_shift_g(row, carry):
        shift_row(shifted_g, row)
        shift_row(shifted_g, 11 + row)
        return carry

    def rim_conv_g(chunk, carry):
        conv_chunk(shifted_g, taps, True, conv, chunk, RIM_PAIRS, None)
        return carry

    lax.fori_loop(0, 3, rim_shift_g, 0)
    schedule.tick(0.6)
    lax.fori_loop(0, 8, rim_conv_g, 0)
    schedule.tick(0.8)
    lax.fori_loop(8, 16, rim_conv_g, 0)
    schedule.tick(0.8)
    for copy in halo[2:]:
        copy.wait()
    take_ghosts(ghosts_g)
    for side in range(2):
        partner_side = edge_ref[1, side, face]
        reverse = edge_ref[2, side, face]
        totals = [jnp.zeros((8, CH), F32) for _ in range(3)]
        for a in range(7):
            weights = []
            for offset in range(1, 4):
                weights.append(
                    pick(
                        partner_side,
                        pick(reverse, taps[(6 - a) * 7 + 3 + offset], taps[a * 7 + 3 + offset]),
                        pick(reverse, taps[(6 - a) * 7 + 3 - offset], taps[a * 7 + 3 - offset]),
                    )
                )
            for other in range(3):
                value = ghost_f[side, other, 11 - a : 19 - a, :]
                for depth in range(3 - other):
                    totals[depth] = totals[depth] + weights[depth + other] * value
        for depth in range(3):
            strip_f[side, 0, depth] = totals[depth]
            col = depth if side == 0 else COLS - 1 - depth
            for row in range(ROWS):
                conv[row, col : col + 1, :] = (
                    conv[row, col : col + 1, :] + strip_f[side, 0, depth, row : row + 1, :]
                )
    schedule.tick(0.5)

    def fields_row(row, carry):
        gfields_ref[row] = (conv[row] + cot_ref[row].astype(F32)).astype(BF16)
        return carry

    lax.fori_loop(0, ROWS, fields_row, 0)
    schedule.tick(0.2)
    schedule.drain()


def copy_out(*refs):
    inputs, outputs, buffers = refs[:7], refs[7:14], refs[14:21]
    in_sem, out_sem = refs[21:]
    pieces = []
    for item in range(7):
        count = 4 if item in (3, 4) else 1
        rows = inputs[item].shape[0] // count
        for part in range(count):
            pieces.append((item, pl.ds(part * rows, rows)))
    arrivals = []
    for index, (item, rows) in enumerate(pieces):
        copy = pltpu.make_async_copy(
            inputs[item].at[rows], buffers[item].at[rows], in_sem.at[index]
        )
        copy.start()
        arrivals.append(copy)
    departures = []
    for index, (item, rows) in enumerate(pieces):
        arrivals[index].wait()
        copy = pltpu.make_async_copy(
            buffers[item].at[rows], outputs[item].at[rows], out_sem.at[index]
        )
        copy.start()
        departures.append(copy)
    for copy in departures:
        copy.wait()


def shards(
    fields,
    cotangent,
    edge_match,
    depth_kernel,
    depth_bias,
    norm_gain,
    norm_bias,
    expand_weight,
    expand_bias,
    reduce_weight,
    reduce_bias,
    layer_scale,
):
    vmem = pl.BlockSpec(memory_space=pltpu.VMEM)
    smem = pl.BlockSpec(memory_space=pltpu.SMEM)
    tile = (16, 128)
    cells = ROWS * COLS
    factor = 1.0 / math.sqrt(FACES * TILES * cells)
    halo_scratch = [
        pltpu.VMEM((2, 2, 3, 8, CH), BF16),
        pltpu.VMEM((3, COLS, CH), BF16),
        pltpu.VMEM((3, COLS, CH), BF16),
        pltpu.VMEM((2, 2, 3, 3, 8, CH), BF16),
    ]
    outputs = pl.pallas_call(
        functools.partial(block_kernel, factor=factor),
        out_shape=(
            jax.ShapeDtypeStruct((ROWS, COLS, CH), BF16),
            jax.ShapeDtypeStruct((ROWS, COLS, CH), BF16),
            jax.ShapeDtypeStruct((7, 7, CH), F32),
            jax.ShapeDtypeStruct((CH, HID), F32),
            jax.ShapeDtypeStruct((HID, CH), F32),
            jax.ShapeDtypeStruct((8, 128), F32),
            jax.ShapeDtypeStruct((5, CH), F32),
        ),
        in_specs=[smem] + [vmem] * 11,
        out_specs=(vmem,) * 7,
        scratch_shapes=[
            pltpu.VMEM((49, 8, CH), F32),
            pltpu.VMEM((14, 144, CH), F32),
            pltpu.VMEM((7, 14, COLS, CH), F32),
            pltpu.VMEM((7, 14, COLS, CH), F32),
            pltpu.VMEM((2, 2, 3, 8, CH), F32),
            *halo_scratch,
            pltpu.VMEM((2, 3, 24, CH), F32),
            pltpu.VMEM((ROWS, COLS, CH), BF16),
            *halo_scratch,
            pltpu.VMEM((ROWS, COLS, CH), F32),
            pltpu.VMEM((ROWS, COLS, CH), F32),
            pltpu.VMEM((ROWS, COLS, 1), F32),
            pltpu.VMEM((cells, CH), BF16),
            pltpu.VMEM((CH + 16, cells), BF16),
            pltpu.VMEM((CH, cells), BF16),
            pltpu.VMEM((cells, HID), F32),
            pltpu.VMEM((cells, HID), BF16),
            pltpu.VMEM((cells, HID), BF16),
            pltpu.VMEM((8, HID), F32),
            pltpu.VMEM((5, 8, CH), F32),
            pltpu.VMEM((4, 2, 32) + tile, BF16),
            pltpu.VMEM((4, 32) + tile, BF16),
            pltpu.VMEM((4, 32) + tile, BF16),
            pltpu.VMEM((4, 15, 2) + tile, BF16),
            pltpu.VMEM((4, 8, 2) + tile, BF16),
            pltpu.VMEM((4, 2, 32) + tile, BF16),
            pltpu.VMEM((16, 8, 128), F32),
            pltpu.VMEM((15, 8, 128), F32),
            pltpu.VMEM((16, 8, 128), F32),
            pltpu.VMEM((16, 8, 128), F32),
            pltpu.SemaphoreType.DMA((14,)),
            pltpu.SemaphoreType.DMA((14,)),
            pltpu.SemaphoreType.DMA((14,)),
            pltpu.SemaphoreType.DMA((14,)),
            pltpu.SemaphoreType.DMA((20,)),
            pltpu.SemaphoreType.DMA((20,)),
            pltpu.SemaphoreType.DMA((5,)),
            pltpu.SemaphoreType.DMA((5,)),
        ],
        compiler_params=pltpu.CompilerParams(
            collective_id=0, has_side_effects=True, vmem_limit_bytes=54 * 1024 * 1024
        ),
    )(
        edge_match.transpose(2, 1, 0),
        fields[0],
        cotangent[0],
        depth_kernel,
        depth_bias.reshape(1, CH),
        norm_gain.reshape(1, CH),
        norm_bias.reshape(1, CH),
        expand_weight,
        expand_bias.reshape(1, HID),
        reduce_weight,
        reduce_bias.reshape(1, CH),
        layer_scale.reshape(1, CH),
    )
    anywhere = pl.BlockSpec(memory_space=pl.ANY)
    result, gfields, gkernel, gexpand, greduce, gbias, gvectors = pl.pallas_call(
        copy_out,
        out_shape=tuple(jax.ShapeDtypeStruct(item.shape, item.dtype) for item in outputs),
        in_specs=[anywhere] * 7,
        out_specs=(anywhere,) * 7,
        scratch_shapes=[pltpu.VMEM(item.shape, item.dtype) for item in outputs]
        + [pltpu.SemaphoreType.DMA((13,)), pltpu.SemaphoreType.DMA((13,))],
    )(*outputs)
    return (result[None], gfields[None], gkernel, gexpand, greduce, gbias.reshape(HID), gvectors)


def solution(mesh):
    return jax.shard_map(
        shards,
        mesh=mesh,
        in_specs=(P("face", "tile", None, None),) * 2 + (P(),) * 10,
        out_specs=(P("face", "tile", None, None),) * 2 + (P(),) * 5,
        check_vma=False,
    )
```

```python
import functools
import math

import jax
import jax.numpy as jnp
from jax import lax
from jax.experimental import pallas as pl
from jax.experimental.pallas import tpu as pltpu
from jax.sharding import PartitionSpec as P

EPSILON = 1e-06
ROOT_COEF = 0.7978845608028654
CUBIC_COEF = 0.044715
MESH = pl.DeviceIdType.MESH
FACES = 8
TILES = 32
ROWS = 8
COLS = 128
CH = 256
HID = 1024
F32 = jnp.float32
BF16 = jnp.bfloat16
OWN_PAIRS = [(i, a) for i in range(ROWS) for a in range(7) if 3 <= i + a <= 10]
RIM_PAIRS = [(i, a) for i in range(ROWS) for a in range(7) if not 3 <= i + a <= 10]


def halo_plan(face, tile):
    beside = face + 1 - 2 * lax.rem(face, 2)
    across = lax.rem(face + 4, FACES)
    plan = [
        ("up", (face, lax.rem(tile + TILES - 1, TILES))),
        ("down", (face, lax.rem(tile + 1, TILES))),
    ]
    for link, partner in enumerate((beside, across)):
        for flip in range(2):
            for place in range(3):
                if flip == 0:
                    target = tile + TILES + 1 - place
                else:
                    target = 2 * TILES - tile - place
                plan.append(((link, flip, place), (partner, lax.rem(target, TILES))))
    return plan


def device_at(x, y, z, core):
    return (2 * y + lax.rem(x, 2), 16 * lax.div(x, 2) + 2 * z + core)


class Schedule:
    def __init__(self):
        self.now = 0.0
        self.flows = []

    def add(self, steps, delays):
        self.flows.append([self.now, list(steps), list(delays)])
        self.tick(0.0)

    def step(self, flow):
        flow[1].pop(0)()
        self.now += 0.3
        if flow[1]:
            flow[0] = self.now + 2.4 * flow[2].pop(0)
        else:
            self.flows.remove(flow)

    def tick(self, cost):
        self.now += 1.25 * cost
        while self.flows:
            flow = min(self.flows, key=lambda item: item[0])
            if flow[0] > self.now:
                break
            self.step(flow)

    def drain(self):
        while self.flows:
            flow = min(self.flows, key=lambda item: item[0])
            self.now = max(self.now, flow[0])
            self.step(flow)


def pick(flag, if_one, if_zero):
    return jnp.where(jnp.broadcast_to(flag, if_one.shape) == 1, if_one, if_zero)


def dot_nn(left, right):
    return lax.dot_general(left, right, (((1,), (0,)), ((), ())), preferred_element_type=F32)


def dot_nt(left, right):
    return lax.dot_general(left, right, (((1,), (1,)), ((), ())), preferred_element_type=F32)


def fold(block):
    return jnp.sum(block.reshape(16, 8, block.shape[1]), axis=0)


def conv_chunk(shifted, taps, flipped, out, chunk, pairs, start):
    cols = pl.ds(pl.multiple_of(chunk * 8, 8), 8)
    for half in range(2):
        lanes = slice(half * 128, half * 128 + 128)
        acc = {}
        for i in sorted({i for i, _ in pairs}):
            acc[i] = out[i, cols, lanes] if start is None else start[:, lanes]
        for b in range(7):
            rows = {r: shifted[b, r, cols, lanes] for r in sorted({i + a for i, a in pairs})}
            for a in sorted({a for _, a in pairs}):
                tap = taps[48 - a * 7 - b if flipped else a * 7 + b, :, lanes]
                for i in sorted({i for i, a2 in pairs if a2 == a}):
                    acc[i] = acc[i] + tap * rows[i + a]
        for i, value in acc.items():
            out[i, cols, lanes] = value


def block_kernel(
    edge_ref,
    fields_ref,
    cot_ref,
    taps_ref,
    depth_bias_ref,
    gain_ref,
    norm_bias_ref,
    w1_ref,
    b1_ref,
    w2_ref,
    b2_ref,
    scale_ref,
    result_ref,
    gfields_ref,
    gkernel_ref,
    gexpand_ref,
    greduce_ref,
    gbias_ref,
    gvectors_ref,
    taps,
    wide,
    shifted,
    shifted_g,
    strip_f,
    strips,
    above,
    below,
    ghosts,
    ghost_f,
    rows_g,
    strips_g,
    above_g,
    below_g,
    ghosts_g,
    conv,
    standard,
    inverse,
    normed,
    normed_t,
    cot_branch_t,
    grad_hidden,
    active,
    grad_pre,
    bias_sum,
    vector_sum,
    src,
    from_core,
    sum_core,
    from_plane,
    sum_z,
    gathered,
    small_in,
    small_plane,
    small_line,
    small_out,
    halo_send,
    halo_recv,
    grad_send,
    grad_recv,
    big_send,
    big_recv,
    small_send,
    small_recv,
    factor,
):
    face, tile = lax.axis_index("face"), lax.axis_index("tile")
    core = lax.rem(tile, 2)
    z = lax.rem(lax.div(tile, 2), 8)
    x = 2 * lax.div(tile, 16) + lax.rem(face, 2)
    y = lax.div(face, 2)
    sibling = device_at(x, y, z, 1 - core)

    mine = 4 * x + y
    lane = 2 * z + core

    def plane_place(step):
        return lax.rem(x + step // 4, 4), lax.rem(y + step % 4, 4)

    def plane_peer(step):
        new_x, new_y = plane_place(step)
        return device_at(new_x, new_y, z, core)

    def z_peer(step):
        return device_at(x, y, lax.rem(z + step, 8), core)

    def line_peer(step):
        new = lax.rem(lane + step, 16)
        return device_at(x, y, lax.div(new, 2), lax.rem(new, 2))

    plan = halo_plan(face, tile)
    barrier = pltpu.get_barrier_semaphore()
    peers = [target for _, target in plan]
    peers += [plane_peer(step) for step in range(1, 16)]
    peers += [line_peer(step) for step in range(1, 16)]
    for peer in peers:
        pl.semaphore_signal(barrier, inc=1, device_id=peer, device_id_type=MESH)

    first = jnp.where(tile == 0, 1, 0)
    last = jnp.where(tile == TILES - 1, 1, 0)
    beside = face + 1 - 2 * lax.rem(face, 2)
    beside_side = jnp.where(edge_ref[0, 0, face] == beside, 0, 1)

    def make_strips(target):
        for row in range(ROWS):
            for depth in range(3):
                for side, col in ((0, 8 + depth), (1, 135 - depth)):
                    piece = wide[3 + row, col : col + 1, :]
                    strip_f[side, 0, depth, row : row + 1, :] = piece
                    strip_f[side, 1, depth, 7 - row : 8 - row, :] = piece
        for flip in range(2):
            for depth in range(3):
                west, east = strip_f[0, flip, depth], strip_f[1, flip, depth]
                target[0, flip, depth] = pick(beside_side, east, west).astype(BF16)
                target[1, flip, depth] = pick(beside_side, west, east).astype(BF16)

    def start_halo(rows, strip, to_above, to_below, to_ghosts, send, recv):
        copies = []
        for index in sorted(range(14), key=lambda i: (i < 2, i < 14 and i >= 2 and plan[i][0][1] == 0)):
            kind, target = plan[index]
            if kind == "up":
                source, landing = rows.at[0:3], to_below
            elif kind == "down":
                source, landing = rows.at[ROWS - 3 : ROWS], to_above
            else:
                link, flip, place = kind
                source, landing = strip.at[link, flip], to_ghosts.at[link, flip, place]
            copy = pltpu.make_async_remote_copy(
                source, landing, send.at[index], recv.at[index], target, MESH
            )
            copy.start()
            copies.append((index, copy))
        return [copy for _, copy in sorted(copies, key=lambda item: item[0])]

    def take_ghosts(source):
        for side in range(2):
            reverse = edge_ref[2, side, face]
            other = beside_side if side == 0 else 1 - beside_side
            for place in range(3):
                for depth in range(3):
                    values = [
                        pick(
                            other,
                            source[1, flip, place, depth].astype(F32),
                            source[0, flip, place, depth].astype(F32),
                        )
                        for flip in range(2)
                    ]
                    value = pick(reverse, values[1], values[0])
                    if place == 0:
                        value = pick(first, jnp.zeros_like(value), value)
                    if place == 2:
                        value = pick(last, jnp.zeros_like(value), value)
                    ghost_f[side, depth, place * 8 : place * 8 + 8, :] = value

    def take_rows(source_above, source_below):
        for row in range(3):
            value = source_above[row].astype(F32)
            wide[row, 8:136, :] = pick(first, jnp.zeros_like(value), value)
            value = source_below[row].astype(F32)
            wide[11 + row, 8:136, :] = pick(last, jnp.zeros_like(value), value)

    def shift_row(target, row):
        for b in range(7):
            target[b, row] = wide[row, 5 + b : 133 + b, :]

    for a in range(7):
        block = taps_ref[a].astype(F32)
        for b in range(7):
            taps[a * 7 + b] = jnp.broadcast_to(block[b : b + 1, :], (8, CH))
    edge_zero = jnp.zeros((8, CH), F32)

    def load_row(row, carry):
        wide[3 + row, 0:8, :] = edge_zero
        wide[3 + row, 136:144, :] = edge_zero
        wide[3 + row, 8:136, :] = fields_ref[row].astype(F32)
        return carry

    lax.fori_loop(0, ROWS, load_row, 0)
    make_strips(strips)
    vector_sum[...] = jnp.zeros_like(vector_sum)

    def own_shift(row, carry):
        shift_row(shifted, 3 + row)
        return carry

    lax.fori_loop(0, ROWS, own_shift, 0)
    def cot_row(row, carry):
        cells = pl.ds(pl.multiple_of(row * COLS, COLS), COLS)
        upstream = cot_ref[row].astype(F32)
        scaled = upstream * scale_ref[...]
        half_grad = (0.5 * scaled).astype(BF16)
        cot_branch_t[:, cells] = jnp.transpose(scaled).astype(BF16)
        vector_sum[3] = vector_sum[3] + fold(upstream)
        for part in range(4):
            hidden = slice(part * 256, part * 256 + 256)
            grad_hidden[cells, hidden] = dot_nt(half_grad, w2_ref[hidden, :])
        return carry

    lax.fori_loop(0, ROWS, cot_row, 0)
    pl.semaphore_wait(barrier, len(peers))
    halo = start_halo(fields_ref, strips, above, below, ghosts, halo_send, halo_recv)

    start = jnp.broadcast_to(depth_bias_ref[...], (8, CH))

    def own_conv(chunk, carry):
        conv_chunk(shifted, taps, False, conv, chunk, OWN_PAIRS, start)
        return carry

    lax.fori_loop(1, 15, own_conv, 0)

    halo[0].wait()
    halo[1].wait()
    take_rows(above, below)

    def rim_shift(row, carry):
        shift_row(shifted, row)
        shift_row(shifted, 11 + row)
        return carry

    lax.fori_loop(0, 3, rim_shift, 0)

    def rim_conv(chunk, carry):
        conv_chunk(shifted, taps, False, conv, chunk, RIM_PAIRS, None)
        return carry

    lax.fori_loop(1, 15, rim_conv, 0)
    for copy in halo[2:]:
        copy.wait()
    take_ghosts(ghosts)
    for row in range(14):
        for depth in range(3):
            wide[row, 7 - depth : 8 - depth, :] = ghost_f[0, depth, row + 5 : row + 6, :]
            wide[row, 136 + depth : 137 + depth, :] = ghost_f[1, depth, row + 5 : row + 6, :]

    def edge_shift(row, carry):
        for b in range(7):
            shifted[b, row, 0:8, :] = wide[row, 5 + b : 13 + b, :]
            shifted[b, row, 120:128, :] = wide[row, 125 + b : 133 + b, :]
        return carry

    lax.fori_loop(0, 14, edge_shift, 0)

    def edge_conv(index, carry):
        conv_chunk(shifted, taps, False, conv, index * 15, OWN_PAIRS + RIM_PAIRS, start)
        return carry

    lax.fori_loop(0, 2, edge_conv, 0)

    normed_t[256:272, :] = jnp.ones((16, ROWS * COLS), BF16)

    def norm_row(row, carry):
        cells = pl.ds(pl.multiple_of(row * COLS, COLS), COLS)
        value = conv[row]
        centred = value - jnp.sum(value, axis=1, keepdims=True) * (1.0 / CH)
        variance = jnp.sum(centred * centred, axis=1, keepdims=True) * (1.0 / CH)
        inv = lax.rsqrt(variance + EPSILON)
        std = centred * inv
        standard[row] = std
        inverse[row] = inv
        scaled = std * gain_ref[...] + norm_bias_ref[...]
        normed[cells, :] = (0.5 * scaled).astype(BF16)
        normed_t[0:256, cells] = jnp.transpose(scaled).astype(BF16)
        return carry

    lax.fori_loop(0, ROWS, norm_row, 0)

    schedule = Schedule()

    def part_flow(part):
        counter = [part * 5]
        def send(source, landing, target):
            pltpu.make_async_remote_copy(
                source,
                landing,
                big_send.at[counter[0]],
                big_recv.at[counter[0]],
                target,
                MESH,
            ).start()

        def arrived(like):
            every = pltpu.make_async_remote_copy(
                like, like, big_send.at[counter[0]], big_recv.at[counter[0]], sibling, MESH
            )
            every.wait_send()
            every.wait_recv()
            counter[0] += 1

        def to_core():
            send(src.at[part, 1 - core], from_core.at[part], sibling)

        def to_plane():
            arrived(from_core.at[part])

            def add(index, carry):
                sum_core[part, index] = (
                    src[part, core, index].astype(F32) + from_core[part, index].astype(F32)
                ).astype(BF16)
                return carry

            lax.fori_loop(0, 32, add, 0, unroll=8)
            for step in range(1, 16):
                new_x, new_y = plane_place(step)
                block = sum_core.at[part, pl.ds(8 * new_x + 2 * new_y, 2)]
                send(block, from_plane.at[part, step - 1], plane_peer(step))

        def to_z():
            arrived(from_plane.at[part])
            for index in range(2):
                total = sum_core[part, 2 * mine + index].astype(F32)
                for step in range(15):
                    total = total + from_plane[part, step, index].astype(F32)
                sum_z[part, z, index] = total.astype(BF16)
            for step in range(1, 8):
                send(sum_z.at[part, z], sum_z.at[part, z], z_peer(step))

        def back_plane():
            arrived(sum_z.at[part, 0:7])
            for index in range(2):
                total = sum_z[part, 0, index].astype(F32)
                for step in range(1, 8):
                    total = total + sum_z[part, step, index].astype(F32)
                gathered[part, core, 2 * mine + index] = total.astype(BF16)
            block = gathered.at[part, core, pl.ds(2 * mine, 2)]
            for step in range(1, 16):
                send(block, block, plane_peer(step))

        def back_core():
            arrived(from_plane.at[part])
            send(gathered.at[part, core], gathered.at[part, core], sibling)

        def unpack():
            arrived(gathered.at[part, core])

            def one(row, carry):
                rows = pl.ds(pl.multiple_of(row * 16, 16), 16)
                down = pl.ds(pl.multiple_of(part * 256 + row * 16, 16), 16)
                for col in range(2):
                    across = slice(part * 256 + col * 128, part * 256 + col * 128 + 128)
                    lanes = slice(col * 128, col * 128 + 128)
                    gexpand_ref[rows, across] = gathered[part, 0, row * 2 + col].astype(F32) * factor
                    greduce_ref[down, lanes] = gathered[part, 1, row * 2 + col].astype(F32) * factor
                return carry

            lax.fori_loop(0, 16, one, 0, unroll=4)

        schedule.add(
            [to_core, to_plane, to_z, back_plane, back_core, unpack],
            [1.7, 5.6, 5.6, 5.6, 1.7],
        )

    for part in range(4):
        hidden = slice(part * 256, part * 256 + 256)

        def hidden_row(row, carry):
            cells = pl.ds(pl.multiple_of(row * 512, 512), 512)
            half = dot_nn(normed[cells, :], w1_ref[:, hidden]) + 0.5 * b1_ref[:, hidden]
            square = half * half
            tanhed = jnp.tanh(
                half * (2.0 * ROOT_COEF + (8.0 * ROOT_COEF * CUBIC_COEF) * square)
            )
            plus = 1.0 + tanhed
            value = half * plus
            active[cells, hidden] = value.astype(BF16)
            twice_slope = plus + (value * (1.0 - tanhed)) * (
                2.0 * ROOT_COEF + (24.0 * ROOT_COEF * CUBIC_COEF) * square
            )
            grad_pre[cells, hidden] = (grad_hidden[cells, hidden] * twice_slope).astype(BF16)
            return carry

        lax.fori_loop(0, 1, hidden_row, 0)
        schedule.tick(0.7)
        lax.fori_loop(1, 2, hidden_row, 0)
        schedule.tick(0.7)
        block = dot_nn(normed_t[...], grad_pre[:, hidden])
        bias_sum[:, hidden] = block[256:264, :]
        block = block[0:256, :].astype(BF16)
        for row in range(16):
            for col in range(2):
                src[part, 0, row * 2 + col] = block[
                    row * 16 : row * 16 + 16, col * 128 : col * 128 + 128
                ]
        schedule.tick(0.3)
        block = jnp.transpose(dot_nn(cot_branch_t[...], active[:, hidden])).astype(BF16)
        for row in range(16):
            for col in range(2):
                src[part, 1, row * 2 + col] = block[
                    row * 16 : row * 16 + 16, col * 128 : col * 128 + 128
                ]
        schedule.tick(0.3)
        part_flow(part)

    def grad_row(pair, carry):
        both = dot_nt(grad_pre[pl.ds(pl.multiple_of(pair * 256, 256), 256), :], w1_ref[...])
        for side in range(2):
            row = pair * 2 + side
            grad_normed = both[side * 128 : side * 128 + 128]
            std = standard[row]
            scaled = grad_normed * gain_ref[...]
            mean = jnp.sum(scaled, axis=1, keepdims=True) * (1.0 / CH)
            slant = jnp.sum(scaled * std, axis=1, keepdims=True) * (1.0 / CH)
            grad = (scaled - mean - std * slant) * inverse[row]
            conv[row] = grad
            wide[3 + row, 0:8, :] = edge_zero
            wide[3 + row, 136:144, :] = edge_zero
            wide[3 + row, 8:136, :] = grad
            rows_g[row] = grad.astype(BF16)
            vector_sum[0] = vector_sum[0] + fold(grad)
            vector_sum[1] = vector_sum[1] + fold(grad_normed * std)
            vector_sum[2] = vector_sum[2] + fold(grad_normed)
        return carry

    lax.fori_loop(0, 2, grad_row, 0)
    schedule.tick(0.9)
    lax.fori_loop(2, 4, grad_row, 0)
    make_strips(strips_g)
    halo = start_halo(rows_g, strips_g, above_g, below_g, ghosts_g, grad_send, grad_recv)
    schedule.tick(1.0)

    def result_row(pair, carry):
        both = dot_nn(active[pl.ds(pl.multiple_of(pair * 256, 256), 256), :], w2_ref[...])
        for side in range(2):
            row = pair * 2 + side
            branch = both[side * 128 : side * 128 + 128] + b2_ref[...]
            result_ref[row] = (fields_ref[row].astype(F32) + scale_ref[...] * branch).astype(BF16)
            vector_sum[4] = vector_sum[4] + fold(cot_ref[row].astype(F32) * branch)
        return carry

    lax.fori_loop(0, 2, result_row, 0)
    schedule.tick(0.6)
    lax.fori_loop(2, 4, result_row, 0)
    schedule.tick(0.6)

    small_in[...] = jnp.zeros_like(small_in)
    for b in range(7):

        def tap_sums(chunk, carry):
            cols = pl.ds(pl.multiple_of(chunk * 8, 8), 8)
            sums = list(carry)
            for half in range(2):
                lanes = slice(half * 128, half * 128 + 128)
                grads = [conv[i, cols, lanes] for i in range(ROWS)]
                for r in range(14):
                    value = shifted[b, r, cols, lanes]
                    for a in range(7):
                        if 0 <= r - a < ROWS:
                            sums[a * 2 + half] = sums[a * 2 + half] + grads[r - a] * value
            return tuple(sums)

        sums = lax.fori_loop(0, 16, tap_sums, tuple(jnp.zeros((8, 128), F32) for _ in range(14)))
        for index, value in enumerate(sums):
            small_in[index, b : b + 1, :] = jnp.sum(value, axis=0, keepdims=True)
        schedule.tick(0.85)
    for part in range(8):
        small_in[part, 7:8, :] = bias_sum[0:1, part * 128 : part * 128 + 128]
    for row in range(5):
        total = jnp.sum(vector_sum[row], axis=0, keepdims=True)
        if row == 3:
            total = total * scale_ref[...]
        for half in range(2):
            small_in[14 + half, row : row + 1, :] = total[:, half * 128 : half * 128 + 128]

    def small_flow():
        counter = [0]

        def send(source, landing, target):
            pltpu.make_async_remote_copy(
                source,
                landing,
                small_send.at[counter[0]],
                small_recv.at[counter[0]],
                target,
                MESH,
            ).start()

        def arrived(like):
            every = pltpu.make_async_remote_copy(
                like, like, small_send.at[counter[0]], small_recv.at[counter[0]], sibling, MESH
            )
            every.wait_send()
            every.wait_recv()
            counter[0] += 1

        def to_plane():
            for step in range(1, 16):
                new_x, new_y = plane_place(step)
                send(small_in.at[4 * new_x + new_y], small_plane.at[step - 1], plane_peer(step))

        def to_line():
            arrived(small_plane)
            total = small_in[mine]
            for step in range(15):
                total = total + small_plane[step]
            small_line[lane] = total
            for step in range(1, 16):
                send(small_line.at[lane], small_line.at[lane], line_peer(step))

        def back_plane():
            arrived(small_plane)
            total = small_line[0]
            for step in range(1, 16):
                total = total + small_line[step]
            small_out[mine] = total * factor
            for step in range(1, 16):
                send(small_out.at[mine], small_out.at[mine], plane_peer(step))

        def unpack():
            arrived(small_plane)
            for a in range(7):
                for half in range(2):
                    lanes = slice(half * 128, half * 128 + 128)
                    gkernel_ref[a, :, lanes] = small_out[2 * a + half, 0:7, :]
            for part in range(8):
                gbias_ref[part : part + 1, :] = small_out[part, 7:8, :]
            for half in range(2):
                lanes = slice(half * 128, half * 128 + 128)
                gvectors_ref[:, lanes] = small_out[14 + half, 0:5, :]

        schedule.add(
            [to_plane, to_line, back_plane, unpack], [5.0, 5.5, 5.0]
        )

    small_flow()

    def own_shift_g(row, carry):
        shift_row(shifted_g, 3 + row)
        return carry

    def own_conv_g(chunk, carry):
        conv_chunk(shifted_g, taps, True, conv, chunk, OWN_PAIRS, edge_zero)
        return carry

    lax.fori_loop(0, ROWS, own_shift_g, 0)
    schedule.tick(0.65)
    for quarter in range(4):
        lax.fori_loop(quarter * 4, quarter * 4 + 4, own_conv_g, 0)
        schedule.tick(1.1)
    halo[0].wait()
    halo[1].wait()
    take_rows(above_g, below_g)
    for row in range(3):
        for side_row in (row, 11 + row):
            wide[side_row, 0:8, :] = edge_zero
            wide[side_row, 136:144, :] = edge_zero

    def rim_shift_g(row, carry):
        shift_row(shifted_g, row)
        shift_row(shifted_g, 11 + row)
        return carry

    def rim_conv_g(chunk, carry):
        conv_chunk(shifted_g, taps, True, conv, chunk, RIM_PAIRS, None)
        return carry

    lax.fori_loop(0, 3, rim_shift_g, 0)
    schedule.tick(0.6)
    lax.fori_loop(0, 8, rim_conv_g, 0)
    schedule.tick(0.8)
    lax.fori_loop(8, 16, rim_conv_g, 0)
    schedule.tick(0.8)
    for copy in halo[2:]:
        copy.wait()
    take_ghosts(ghosts_g)
    for side in range(2):
        partner_side = edge_ref[1, side, face]
        reverse = edge_ref[2, side, face]
        totals = [jnp.zeros((8, CH), F32) for _ in range(3)]
        for a in range(7):
            weights = []
            for offset in range(1, 4):
                weights.append(
                    pick(
                        partner_side,
                        pick(reverse, taps[(6 - a) * 7 + 3 + offset], taps[a * 7 + 3 + offset]),
                        pick(reverse, taps[(6 - a) * 7 + 3 - offset], taps[a * 7 + 3 - offset]),
                    )
                )
            for other in range(3):
                value = ghost_f[side, other, 11 - a : 19 - a, :]
                for depth in range(3 - other):
                    totals[depth] = totals[depth] + weights[depth + other] * value
        for depth in range(3):
            strip_f[side, 0, depth] = totals[depth]
            col = depth if side == 0 else COLS - 1 - depth
            for row in range(ROWS):
                conv[row, col : col + 1, :] = (
                    conv[row, col : col + 1, :] + strip_f[side, 0, depth, row : row + 1, :]
                )
    schedule.tick(0.5)

    def fields_row(row, carry):
        gfields_ref[row] = (conv[row] + cot_ref[row].astype(F32)).astype(BF16)
        return carry

    lax.fori_loop(0, ROWS, fields_row, 0)
    schedule.tick(0.2)
    schedule.drain()


def copy_out(*refs):
    inputs, outputs, buffers = refs[:7], refs[7:14], refs[14:21]
    in_sem, out_sem = refs[21:]
    pieces = []
    for item in range(7):
        count = 4 if item in (3, 4) else 1
        rows = inputs[item].shape[0] // count
        for part in range(count):
            pieces.append((item, pl.ds(part * rows, rows)))
    arrivals = []
    for index, (item, rows) in enumerate(pieces):
        copy = pltpu.make_async_copy(
            inputs[item].at[rows], buffers[item].at[rows], in_sem.at[index]
        )
        copy.start()
        arrivals.append(copy)
    departures = []
    for index, (item, rows) in enumerate(pieces):
        arrivals[index].wait()
        copy = pltpu.make_async_copy(
            buffers[item].at[rows], outputs[item].at[rows], out_sem.at[index]
        )
        copy.start()
        departures.append(copy)
    for copy in departures:
        copy.wait()


def shards(
    fields,
    cotangent,
    edge_match,
    depth_kernel,
    depth_bias,
    norm_gain,
    norm_bias,
    expand_weight,
    expand_bias,
    reduce_weight,
    reduce_bias,
    layer_scale,
):
    vmem = pl.BlockSpec(memory_space=pltpu.VMEM)
    smem = pl.BlockSpec(memory_space=pltpu.SMEM)
    tile = (16, 128)
    cells = ROWS * COLS
    factor = 1.0 / math.sqrt(FACES * TILES * cells)
    halo_scratch = [
        pltpu.VMEM((2, 2, 3, 8, CH), BF16),
        pltpu.VMEM((3, COLS, CH), BF16),
        pltpu.VMEM((3, COLS, CH), BF16),
        pltpu.VMEM((2, 2, 3, 3, 8, CH), BF16),
    ]
    outputs = pl.pallas_call(
        functools.partial(block_kernel, factor=factor),
        out_shape=(
            jax.ShapeDtypeStruct((ROWS, COLS, CH), BF16),
            jax.ShapeDtypeStruct((ROWS, COLS, CH), BF16),
            jax.ShapeDtypeStruct((7, 7, CH), F32),
            jax.ShapeDtypeStruct((CH, HID), F32),
            jax.ShapeDtypeStruct((HID, CH), F32),
            jax.ShapeDtypeStruct((8, 128), F32),
            jax.ShapeDtypeStruct((5, CH), F32),
        ),
        in_specs=[smem] + [vmem] * 11,
        out_specs=(vmem,) * 7,
        scratch_shapes=[
            pltpu.VMEM((49, 8, CH), F32),
            pltpu.VMEM((14, 144, CH), F32),
            pltpu.VMEM((7, 14, COLS, CH), F32),
            pltpu.VMEM((7, 14, COLS, CH), F32),
            pltpu.VMEM((2, 2, 3, 8, CH), F32),
            *halo_scratch,
            pltpu.VMEM((2, 3, 24, CH), F32),
            pltpu.VMEM((ROWS, COLS, CH), BF16),
            *halo_scratch,
            pltpu.VMEM((ROWS, COLS, CH), F32),
            pltpu.VMEM((ROWS, COLS, CH), F32),
            pltpu.VMEM((ROWS, COLS, 1), F32),
            pltpu.VMEM((cells, CH), BF16),
            pltpu.VMEM((CH + 16, cells), BF16),
            pltpu.VMEM((CH, cells), BF16),
            pltpu.VMEM((cells, HID), F32),
            pltpu.VMEM((cells, HID), BF16),
            pltpu.VMEM((cells, HID), BF16),
            pltpu.VMEM((8, HID), F32),
            pltpu.VMEM((5, 8, CH), F32),
            pltpu.VMEM((4, 2, 32) + tile, BF16),
            pltpu.VMEM((4, 32) + tile, BF16),
            pltpu.VMEM((4, 32) + tile, BF16),
            pltpu.VMEM((4, 15, 2) + tile, BF16),
            pltpu.VMEM((4, 8, 2) + tile, BF16),
            pltpu.VMEM((4, 2, 32) + tile, BF16),
            pltpu.VMEM((16, 8, 128), F32),
            pltpu.VMEM((15, 8, 128), F32),
            pltpu.VMEM((16, 8, 128), F32),
            pltpu.VMEM((16, 8, 128), F32),
            pltpu.SemaphoreType.DMA((14,)),
            pltpu.SemaphoreType.DMA((14,)),
            pltpu.SemaphoreType.DMA((14,)),
            pltpu.SemaphoreType.DMA((14,)),
            pltpu.SemaphoreType.DMA((20,)),
            pltpu.SemaphoreType.DMA((20,)),
            pltpu.SemaphoreType.DMA((5,)),
            pltpu.SemaphoreType.DMA((5,)),
        ],
        compiler_params=pltpu.CompilerParams(
            collective_id=0, has_side_effects=True, vmem_limit_bytes=54 * 1024 * 1024
        ),
    )(
        edge_match.transpose(2, 1, 0),
        fields[0],
        cotangent[0],
        depth_kernel,
        depth_bias.reshape(1, CH),
        norm_gain.reshape(1, CH),
        norm_bias.reshape(1, CH),
        expand_weight,
        expand_bias.reshape(1, HID),
        reduce_weight,
        reduce_bias.reshape(1, CH),
        layer_scale.reshape(1, CH),
    )
    anywhere = pl.BlockSpec(memory_space=pl.ANY)
    result, gfields, gkernel, gexpand, greduce, gbias, gvectors = pl.pallas_call(
        copy_out,
        out_shape=tuple(jax.ShapeDtypeStruct(item.shape, item.dtype) for item in outputs),
        in_specs=[anywhere] * 7,
        out_specs=(anywhere,) * 7,
        scratch_shapes=[pltpu.VMEM(item.shape, item.dtype) for item in outputs]
        + [pltpu.SemaphoreType.DMA((13,)), pltpu.SemaphoreType.DMA((13,))],
    )(*outputs)
    return (result[None], gfields[None], gkernel, gexpand, greduce, gbias.reshape(HID), gvectors)


def solution(mesh):
    return jax.shard_map(
        shards,
        mesh=mesh,
        in_specs=(P("face", "tile", None, None),) * 2 + (P(),) * 10,
        out_specs=(P("face", "tile", None, None),) * 2 + (P(),) * 5,
        check_vma=False,
    )
```
